256 devices in a mesh: req: 32 (over x, y, core), kv: 8 (over z).
Axes of the slice: x: 4, y: 4, z: 8, core: 2. Of those that a mesh axis runs over, the one named last changes fastest.
Arguments:
- queries: bfloat16 [256, 4096], P(('req', 'kv')), may hold values from -16 to 16
- paged_key_cache: bfloat16 [1536, 128, 1024], P(('req', 'kv')), may hold values from -8 to 8
- paged_value_cache: bfloat16 [1536, 128, 1024], P(('req', 'kv')), may hold values from -6 to 6
- page_request: int32 [1536], P(('req', 'kv')), may hold values from 0 to 255, as said below
- page_number: int32 [1536], P(('req', 'kv')), may hold values from 0 to 23, as said below
- lengths: int32 [256], replicated, may hold values from 1 to 3072, as said below
Outputs:
- attended: bfloat16 [256, 4096], P(('req', 'kv'))
The draws below stay inside these ranges and needn't reach their ends.
Inputs may be any that keep to these rules, and one draw needn't show every extreme that they name: `page_request`: every request has 1 to 24 pages and some request exactly 24; the 6 slots of one device hold pages of requests r with 6 different values of r // 8. `page_number`: the pages of one request are numbered 0, 1, 2 and so on without gaps, each number once. `lengths`: a request with n pages has a length from (n - 1) * 128 + 1 to n * 128.
All inputs are finite; a program needn't handle non-finite values.
Results may differ from the reference program's by a relative error of at most 0.0023.
Values may be sent and summed in bfloat16 or wider, within the bound.
No kernel may reach another device: no remote copies, remote signals or barrier semaphores. Data moves between devices by JAX's collectives and lax.ppermute only.
A program may use at most 64 MiB of HBM per device.

```python
import jax
import jax.numpy as jnp
from jax import lax

HQ = 32
KEY_VALUE_HEADS = 8
HEAD_SIZE = 128
PAGE_TOKENS = 128
DEVICE_PAGES = 6
QUERY_PER_KV = 4
REQUESTS = 256
TOTAL_PAGES = 1536
MOST_PAGES = 24
DEVICES = 256


def page_tables(key):
    base = jax.random.fold_in(key, 11)
    streams = jax.random.split(base, 7)
    relabel = jax.random.permutation(streams[0], REQUESTS).astype(jnp.int32)
    starts = jax.random.randint(streams[1], (REQUESTS,), 0, 1024).astype(jnp.int32)
    slopes = jax.random.randint(streams[2], (REQUESTS,), 1, 65).astype(jnp.int32)
    forced = relabel[0]
    starts = starts.at[forced].set(4096)
    slopes = slopes.at[forced].set(1)
    cells = REQUESTS * MOST_PAGES
    ranks = jnp.arange(MOST_PAGES, dtype=jnp.int32)
    ties = jax.random.permutation(streams[3], cells).astype(jnp.int32).reshape(REQUESTS, MOST_PAGES)
    score = (starts[:, None] - ranks[None, :] * slopes[:, None]) * cells + ties
    score = jnp.where(ranks[None, :] == 0, 2 ** 30, score).reshape(cells)
    order = jnp.argsort(-score)
    chosen = jnp.zeros((cells,), jnp.int32).at[order[:TOTAL_PAGES]].set(1)
    flat = jnp.arange(cells, dtype=jnp.int32)
    listing = jnp.argsort((1 - chosen) * cells + flat)[:TOTAL_PAGES].astype(jnp.int32)
    request_of = listing // MOST_PAGES
    number_of = listing % MOST_PAGES
    places = jnp.arange(TOTAL_PAGES, dtype=jnp.int32)
    shuffle = jax.random.permutation(streams[4], DEVICES).astype(jnp.int32)
    device = jnp.take(shuffle, places % DEVICES)
    offsets = jax.random.randint(streams[5], (DEVICES,), 0, DEVICE_PAGES).astype(jnp.int32)
    slot = (places // DEVICES + jnp.take(offsets, device)) % DEVICE_PAGES
    position = device * DEVICE_PAGES + slot
    owners = jnp.zeros((TOTAL_PAGES,), jnp.int32).at[position].set(request_of)
    numbers = jnp.zeros((TOTAL_PAGES,), jnp.int32).at[position].set(number_of)
    counts = jnp.sum(chosen.reshape(REQUESTS, MOST_PAGES), axis=1)
    extra = jax.random.randint(streams[6], (REQUESTS,), 1, PAGE_TOKENS + 1)
    request_lengths = ((counts - 1) * PAGE_TOKENS + extra).astype(jnp.int32)
    return (owners, numbers, request_lengths)


def draw_page_request(key, part):
    return page_tables(key)[0]


def draw_page_number(key, part):
    return page_tables(key)[1]


def draw_lengths(key, part):
    return page_tables(key)[2]


def draw_queries(key, part):
    random_noise = jax.random.normal(jax.random.fold_in(key, 21), (REQUESTS, HQ, HEAD_SIZE), jnp.float32)
    result = jnp.clip(2.5 * random_noise, -16.0, 16.0)
    return result.reshape(REQUESTS, HQ * HEAD_SIZE).astype(jnp.bfloat16)


def draw_paged_key_cache(key, part):
    random_noise = jnp.clip(jax.random.normal(jax.random.fold_in(key, 41), (TOTAL_PAGES, PAGE_TOKENS, KEY_VALUE_HEADS, HEAD_SIZE), jnp.float32), -6.0, 6.0)
    return random_noise.reshape(TOTAL_PAGES, PAGE_TOKENS, KEY_VALUE_HEADS * HEAD_SIZE).astype(jnp.bfloat16)


def level_of(stream_key, extent, cuts, least, top_value):
    gain = 1.0
    for axis_at, parts in cuts:
        draws = jax.random.uniform(jax.random.fold_in(jax.random.fold_in(stream_key, 6), axis_at), (parts,), jnp.float32, least / len(cuts), top_value / len(cuts))
        gain = gain * jnp.repeat(jnp.exp(draws), extent[axis_at] // parts).reshape((-1,) + (1,) * (len(extent) - 1 - axis_at))
    return gain


def noise(rng, shape, width, most, cuts=(), kind=jnp.bfloat16):
    drawn = width * jax.random.normal(rng, shape, jnp.float32)
    if cuts:
        drawn = drawn * level_of(rng, shape, cuts, -0.22, 0.18)
    return jnp.clip(drawn, -most, most).astype(kind)


def setup_inputs(seed: int = 0) -> dict:
    key_of = jax.random.split(jax.random.key(seed), 7)
    queries = draw_queries(jax.random.fold_in(key_of[6], 71), 0)
    paged_key_cache = draw_paged_key_cache(jax.random.fold_in(key_of[6], 71), 0)
    paged_value_cache = noise(key_of[2], (TOTAL_PAGES, PAGE_TOKENS, KEY_VALUE_HEADS * HEAD_SIZE), 1.0, 6.0, ((0, 256),))
    page_request = draw_page_request(jax.random.fold_in(key_of[6], 71), 0)
    page_number = draw_page_number(jax.random.fold_in(key_of[6], 71), 0)
    lengths = draw_lengths(jax.random.fold_in(key_of[6], 71), 0)
    return dict(queries=queries, paged_key_cache=paged_key_cache, paged_value_cache=paged_value_cache, page_request=page_request, page_number=page_number, lengths=lengths)


lowest = -1e30


def page_attention(gathered_query_rows, gathered_key_rows, gathered_value_rows, usable):
    token_count = gathered_query_rows.shape[0]
    query_single = gathered_query_rows.astype(jnp.float32).reshape(token_count, KEY_VALUE_HEADS, QUERY_PER_KV, HEAD_SIZE)
    key_single = gathered_key_rows.astype(jnp.float32).reshape(token_count, PAGE_TOKENS, KEY_VALUE_HEADS, HEAD_SIZE)
    value_single = gathered_value_rows.astype(jnp.float32).reshape(token_count, PAGE_TOKENS, KEY_VALUE_HEADS, HEAD_SIZE)
    scores = jnp.einsum("sgqd,stgd->sgqt", query_single, key_single, precision=lax.Precision.HIGHEST) * (HEAD_SIZE ** -0.5)
    scores = jnp.where(usable[:, None, None, :], scores, lowest)
    maxima = jnp.max(scores, axis=-1)
    weights = jnp.exp(scores - maxima[..., None])
    sums_exp = jnp.sum(weights, axis=-1)
    rounded = weights.astype(jnp.bfloat16).astype(jnp.float32)
    partial_out = jnp.einsum("sgqt,stgd->sgqd", rounded, value_single, precision=lax.Precision.HIGHEST)
    return maxima.reshape(token_count, HQ), sums_exp.reshape(token_count, HQ), partial_out.reshape(token_count, HQ * HEAD_SIZE)


def reference(queries, paged_key_cache, paged_value_cache, page_request, page_number, lengths):
    request_blocks = page_request.reshape(DEVICES, DEVICE_PAGES)
    number_blocks = page_number.reshape(DEVICES, DEVICE_PAGES)
    paged_key_blocks = paged_key_cache.reshape(DEVICES, DEVICE_PAGES, PAGE_TOKENS, KEY_VALUE_HEADS * HEAD_SIZE)
    paged_value_blocks = paged_value_cache.reshape(DEVICES, DEVICE_PAGES, PAGE_TOKENS, KEY_VALUE_HEADS * HEAD_SIZE)
    positions = jnp.arange(PAGE_TOKENS, dtype=jnp.int32)

    def per_block(block):
        owners, numbers, gathered_key_rows, gathered_value_rows = block
        gathered_query_rows = jnp.take(queries, owners, axis=0)
        limits = jnp.take(lengths, owners)
        usable = numbers[:, None] * PAGE_TOKENS + positions[None, :] < limits[:, None]
        return page_attention(gathered_query_rows, gathered_key_rows, gathered_value_rows, usable)

    maxima, sums_exp, partial_out = lax.map(per_block, (request_blocks, number_blocks, paged_key_blocks, paged_value_blocks))
    maxima = maxima.reshape(TOTAL_PAGES, HQ)
    sums_exp = sums_exp.reshape(TOTAL_PAGES, HQ)
    partial_out = partial_out.reshape(TOTAL_PAGES, HQ, HEAD_SIZE)
    request_max = jnp.full((REQUESTS, HQ), lowest, jnp.float32).at[page_request].max(maxima)
    factors = jnp.exp(maxima - jnp.take(request_max, page_request, axis=0))
    numerators = jnp.zeros((REQUESTS, HQ, HEAD_SIZE), jnp.float32).at[page_request].add(factors[:, :, None] * partial_out)
    denominators = jnp.zeros((REQUESTS, HQ), jnp.float32).at[page_request].add(factors * sums_exp)
    attended = numerators / denominators[:, :, None]
    return attended.reshape(REQUESTS, HQ * HEAD_SIZE).astype(jnp.bfloat16)
```

```python
import functools

import jax
import jax.numpy as jnp
from jax import lax
from jax.experimental import pallas as pl
from jax.experimental.pallas import tpu as pltpu
from jax.sharding import PartitionSpec as P

HQ = 32
HEAD_SIZE = 128
PAGE = 128
SLOTS = 6
SLOT_ROWS = 8
MESSAGE_ROWS = 40
ABSENT = -2048.0
TOP = 32767.0


def iota(shape, dim):
    return lax.broadcasted_iota(jnp.int32, shape, dim)


def spread_kernel(pages, query, out):
    lane = iota((16, 128), 1)
    even = iota((16, 128), 0) % 2 == 0
    first = (lax.axis_index("req") % 16) * SLOT_ROWS
    ids = jnp.zeros((16, 128), jnp.float32)
    for s in range(SLOTS):
        ids = jnp.where(lane == first + s, pages[s].astype(jnp.float32), ids)
    for h in range(HQ):
        head = query[0:1, h * 128 : (h + 1) * 128].astype(jnp.float32)
        block = jnp.where(even, jnp.broadcast_to(head, (16, 128)), ids)
        out[16 * h : 16 * h + 16, :] = block.astype(jnp.bfloat16)


def select_kernel(recv, out, member):
    rows = recv[...]
    group, plane = lax.axis_index("req"), lax.axis_index("kv")
    at, half = iota((8, 512), 1), iota((8, 512), 0)
    source = at // 2
    pick = (at % 2 == 1) & (source % 8 == plane) & (source // 128 == half)
    ids = jnp.dot(pick.astype(jnp.bfloat16), rows, preferred_element_type=jnp.float32)
    ids = ids.astype(jnp.int32)
    lane = iota((1, 128), 1)
    spots = []
    for n in range(2):
        wanted = ids[n : n + 1, :]
        hot = iota((512, 128), 0) == jnp.broadcast_to(2 * wanted, (512, 128))
        hot = hot.astype(jnp.float32).astype(jnp.bfloat16)
        got = lax.dot_general(
            hot, rows, (((0,), (0,)), ((), ())), preferred_element_type=jnp.float32
        )
        out[128 * n : 128 * n + 128, :] = got.astype(jnp.bfloat16)
        mine = (wanted // 8 == group) & (lane % 8 < SLOTS)
        spots.append(jnp.where(mine, wanted % 8 + 1, 0).astype(jnp.float32))
    dev, lanes = iota((32, 128), 0), iota((32, 128), 1)
    both = jnp.where(dev < 16, spots[0], spots[1])
    own = jnp.where(lanes // 8 == dev % 16, both, 0.0)
    place = jnp.sum(own, axis=1, keepdims=True) - 1.0
    member[...] = jnp.broadcast_to(place, (32, 128))


def coded(out_rows, lse):
    rows = out_rows.shape[0]
    largest = jnp.max(jnp.abs(out_rows), axis=1, keepdims=True)
    power = jnp.ceil(jnp.log2(jnp.maximum(largest, 1e-30)))
    whole = jnp.round(out_rows * (jnp.exp2(-power) * TOP)).astype(jnp.int32).astype(jnp.int16)
    coarse = jnp.round(lse * 16.0)
    fine = jnp.round((lse - coarse * 0.0625) * 524288.0)
    lane = iota((rows, 128), 1)
    stats = jnp.where(lane == 0, coarse, jnp.where(lane == 1, fine, power))
    return whole, jnp.where(lane < 3, stats, 0.0)


def attend_kernel(pages, numbers, lengths, recv, keys, values, out):
    r, c = iota((SLOTS * HQ, 256), 0), iota((SLOTS * HQ, 256), 1)
    order = (c == (r % HQ) * SLOT_ROWS + r // HQ).astype(jnp.float32).astype(jnp.bfloat16)
    query = jnp.dot(order, recv[...], preferred_element_type=jnp.float32)
    upper = iota((8, 128), 0) < 4
    lane = iota((HQ, 128), 1)
    scores = []
    for s in range(SLOTS):
        parts = []
        for i in range(4):
            q = query[s * HQ + 8 * i : s * HQ + 8 * i + 8, :]
            pair = jnp.concatenate([jnp.where(upper, q, 0.0), jnp.where(upper, 0.0, q)], axis=1)
            parts.append(
                lax.dot_general(
                    pair.astype(jnp.bfloat16),
                    keys[s, :, 256 * i : 256 * i + 256],
                    (((1,), (1,)), ((), ())),
                    preferred_element_type=jnp.float32,
                )
            )
        full = jnp.concatenate(parts, axis=0) * HEAD_SIZE**-0.5
        limit = lengths[pages[s]] - numbers[s] * PAGE
        scores.append(jnp.where(lane < limit, full, -1e30))
    scores = jnp.concatenate(scores, axis=0)
    top = jnp.max(scores, axis=1, keepdims=True)
    weights = jnp.exp(scores - top)
    total = jnp.sum(weights, axis=1, keepdims=True)
    rounded = weights.astype(jnp.bfloat16)
    outs = []
    for s in range(SLOTS):
        for i in range(4):
            both = jnp.dot(
                rounded[s * HQ + 8 * i : s * HQ + 8 * i + 8, :],
                values[s, :, 256 * i : 256 * i + 256],
                preferred_element_type=jnp.float32,
            )
            outs.append(jnp.where(upper, both[:, :128], both[:, 128:]))
    outs = jnp.concatenate(outs, axis=0) / total
    whole, stats = coded(outs, top + jnp.log(total))
    out[...] = jnp.zeros(out.shape, jnp.int16)
    for s in range(SLOTS):
        target = pages[s] // 8
        out[target, 0:HQ, :] = whole[s * HQ : s * HQ + HQ, :]
        turned = jnp.transpose(stats[s * HQ : s * HQ + HQ, :])
        tile = jnp.concatenate([turned[0:8, :], jnp.zeros((8, 96), jnp.float32)], axis=1)
        out[target, HQ:MESSAGE_ROWS, :] = tile.astype(jnp.int32).astype(jnp.int16)


def statistics(recv, count):
    tiles = recv[:, HQ:MESSAGE_ROWS, :].astype(jnp.int32).astype(jnp.float32)
    coarse, fine, power = tiles[:, 0, :], tiles[:, 1, :], tiles[:, 2, :]
    lse = coarse * 0.0625 + fine * (1.0 / 524288.0)
    return lse, jnp.exp2(power) * (1.0 / TOP)


def merge_kernel(recv, member, out):
    place = member[...]
    lse, unit = statistics(recv, 32)
    tops, sums = [], []
    peak = jnp.zeros((32, 128), jnp.float32)
    for j in range(8):
        top = jnp.max(jnp.where(place == j, lse, ABSENT), axis=0, keepdims=True)
        tops.append(top)
        peak = jnp.where(place == j, top, peak)
    weight = jnp.where(place >= 0.0, jnp.exp(lse - peak), 0.0)
    total = jnp.ones((32, 128), jnp.float32)
    for j in range(8):
        add = jnp.sum(jnp.where(place == j, weight, 0.0), axis=0, keepdims=True)
        sums.append(add)
        total = jnp.where(place == j, add, total)
    factor = jnp.transpose(weight / total * unit)[0:HQ, :]
    accs = [jnp.zeros((HQ, 128), jnp.float32) for _ in range(8)]
    for g in range(32):
        row = recv[g, 0:HQ, :].astype(jnp.int32).astype(jnp.float32)
        row = row * jnp.broadcast_to(factor[:, g : g + 1], (HQ, 128))
        at = jnp.broadcast_to(place[g : g + 1, :], (HQ, 128))
        accs = [acc + jnp.where(at == j, row, 0.0) for j, acc in enumerate(accs)]
    lses = [
        jnp.where(add > 0.0, top + jnp.log(jnp.maximum(add, 1e-30)), ABSENT)
        for top, add in zip(tops, sums)
    ]
    spare = jnp.zeros((8, 128), jnp.float32)
    for j in range(8):
        largest = jnp.max(jnp.abs(accs[j]), axis=1, keepdims=True)
        power = jnp.ceil(jnp.log2(jnp.maximum(largest, 1e-30)))
        whole = jnp.round(accs[j] * (jnp.exp2(-power) * TOP)).astype(jnp.int32)
        out[j, 0:HQ, :] = whole.astype(jnp.int16)
        coarse = jnp.round(lses[j] * 16.0)
        fine = jnp.round((lses[j] - coarse * 0.0625) * 524288.0)
        turned = jnp.transpose(jnp.broadcast_to(power, (HQ, 128)))[0:8, :]
        turned = jnp.concatenate([turned, jnp.zeros((8, 96), jnp.float32)], axis=1)
        row = iota((8, 128), 0)
        tile = jnp.where(row == 0, coarse, jnp.where(row == 1, fine, turned))
        tile = jnp.where(row < 3, tile, spare)
        out[j, HQ:MESSAGE_ROWS, :] = tile.astype(jnp.int32).astype(jnp.int16)


def finish_kernel(recv, out):
    lse, unit = statistics(recv, 8)
    top = jnp.max(lse, axis=0, keepdims=True)
    weight = jnp.exp(lse - top)
    total = jnp.sum(weight, axis=0, keepdims=True)
    factor = jnp.transpose(weight / total * unit)[0:HQ, :]
    acc = jnp.zeros((HQ, 128), jnp.float32)
    for k in range(8):
        row = recv[k, 0:HQ, :].astype(jnp.int32).astype(jnp.float32)
        acc = acc + row * jnp.broadcast_to(factor[:, k : k + 1], (HQ, 128))
    for h in range(HQ):
        out[0:1, 128 * h : 128 * h + 128] = acc[h : h + 1, :].astype(jnp.bfloat16)


VMEM = pl.BlockSpec(memory_space=pltpu.VMEM)
SMEM = pl.BlockSpec(memory_space=pltpu.SMEM)


def kernel_call(kernel, shapes, specs, name):
    return pl.pallas_call(
        kernel,
        out_shape=shapes,
        in_specs=specs,
        out_specs=jax.tree.map(lambda _: VMEM, shapes),
        name=name,
        compiler_params=pltpu.CompilerParams(vmem_limit_bytes=32 * 1024 * 1024),
    )


def on_device(queries, paged_key_cache, paged_value_cache, page_request, page_number, lengths):
    shape = jax.ShapeDtypeStruct
    sent = kernel_call(spread_kernel, shape((512, 128), jnp.bfloat16), [SMEM, VMEM], "spread")(
        page_request, queries
    )
    heads = lax.all_to_all(sent, ("req", "kv"), 0, 0, tiled=True)
    picked, member = kernel_call(
        select_kernel,
        (shape((256, 128), jnp.bfloat16), shape((32, 128), jnp.float32)),
        [VMEM],
        "select",
    )(heads)
    wanted = lax.all_to_all(picked, "req", 0, 0, tiled=True)
    partial = kernel_call(
        attend_kernel,
        shape((32, MESSAGE_ROWS, 128), jnp.int16),
        [SMEM, SMEM, SMEM, VMEM, VMEM, VMEM],
        "attend",
    )(page_request, page_number, lengths, wanted, paged_key_cache, paged_value_cache)
    partial = lax.all_to_all(partial, "req", 0, 0, tiled=True)
    merged = kernel_call(
        merge_kernel, shape((8, MESSAGE_ROWS, 128), jnp.int16), [VMEM, VMEM], "merge"
    )(partial, member)
    merged = lax.all_to_all(merged, "kv", 0, 0, tiled=True)
    return kernel_call(finish_kernel, shape((1, 4096), jnp.bfloat16), [VMEM], "finish")(merged)


def solution(mesh):
    placed = (
        P(("req", "kv"), None),
        P(("req", "kv"), None, None),
        P(("req", "kv"), None, None),
        P(("req", "kv")),
        P(("req", "kv")),
        P(),
    )
    return jax.shard_map(
        on_device, mesh=mesh, in_specs=placed, out_specs=P(("req", "kv"), None), check_vma=False
    )
```

```python
import jax
import jax.numpy as jnp
from jax import lax
from jax.experimental import pallas as pl
from jax.experimental.pallas import tpu as pltpu
from jax.sharding import PartitionSpec as P

HQ = 32
HEAD_SIZE = 128
PAGE = 128
SLOTS = 6
SLOT_ROWS = 8
MESSAGE_ROWS = 40
ABSENT = -2048.0
TOP = 32767.0


def iota(shape, dim):
    return lax.broadcasted_iota(jnp.int32, shape, dim)


def spread_kernel(pages_in, query_in, out, pages, query, sems):
    first_copy = pltpu.make_async_copy(pages_in, pages, sems.at[0])
    second_copy = pltpu.make_async_copy(query_in, query, sems.at[1])
    first_copy.start()
    second_copy.start()
    first_copy.wait()
    second_copy.wait()
    lane = iota((16, 128), 1)
    even = iota((16, 128), 0) % 2 == 0
    first = (lax.axis_index("req") % 16) * SLOT_ROWS
    ids = jnp.zeros((16, 128), jnp.float32)
    for s in range(SLOTS):
        ids = jnp.where(lane == first + s, pages[s].astype(jnp.float32), ids)
    for h in range(HQ):
        head = query[0:1, h * 128 : (h + 1) * 128].astype(jnp.float32)
        block = jnp.where(even, jnp.broadcast_to(head, (16, 128)), ids)
        out[16 * h : 16 * h + 16, :] = block.astype(jnp.bfloat16)


def select_kernel(recv, out, member):
    rows = recv[...]
    group, plane = lax.axis_index("req"), lax.axis_index("kv")
    at, half = iota((8, 512), 1), iota((8, 512), 0)
    source = at // 2
    pick = (at % 2 == 1) & (source % 8 == plane) & (source // 128 == half)
    ids = jnp.dot(pick.astype(jnp.bfloat16), rows, preferred_element_type=jnp.float32)
    ids = ids.astype(jnp.int32)
    lane = iota((1, 128), 1)
    spots = []
    for n in range(2):
        wanted = ids[n : n + 1, :]
        hot = iota((512, 128), 0) == jnp.broadcast_to(2 * wanted, (512, 128))
        hot = hot.astype(jnp.float32).astype(jnp.bfloat16)
        got = lax.dot_general(
            hot, rows, (((0,), (0,)), ((), ())), preferred_element_type=jnp.float32
        )
        out[128 * n : 128 * n + 128, :] = got.astype(jnp.bfloat16)
        mine = (wanted // 8 == group) & (lane % 8 < SLOTS)
        spots.append(jnp.where(mine, wanted % 8 + 1, 0).astype(jnp.float32))
    dev, lanes = iota((32, 128), 0), iota((32, 128), 1)
    both = jnp.where(dev < 16, spots[0], spots[1])
    own = jnp.where(lanes // 8 == dev % 16, both, 0.0)
    place = jnp.sum(own, axis=1, keepdims=True) - 1.0
    member[...] = jnp.broadcast_to(place, (32, 128))


def coded(out_rows, lse):
    rows = out_rows.shape[0]
    largest = jnp.max(jnp.abs(out_rows), axis=1, keepdims=True)
    power = jnp.ceil(jnp.log2(jnp.maximum(largest, 1e-30)))
    whole = jnp.round(out_rows * (jnp.exp2(-power) * TOP)).astype(jnp.int32).astype(jnp.int16)
    coarse = jnp.round(lse * 16.0)
    fine = jnp.round((lse - coarse * 0.0625) * 524288.0)
    lane = iota((rows, 128), 1)
    stats = jnp.where(lane == 0, coarse, jnp.where(lane == 1, fine, power))
    return whole, jnp.where(lane < 3, stats, 0.0)


def attend_kernel(pages, numbers, lengths, recv, keys, values, out):
    r, c = iota((SLOTS * HQ, 256), 0), iota((SLOTS * HQ, 256), 1)
    order = (c == (r % HQ) * SLOT_ROWS + r // HQ).astype(jnp.float32).astype(jnp.bfloat16)
    query = jnp.dot(order, recv[...], preferred_element_type=jnp.float32)
    upper = iota((8, 128), 0) < 4
    lane = iota((HQ, 128), 1)
    scores = []
    for s in range(SLOTS):
        parts = []
        for i in range(4):
            q = query[s * HQ + 8 * i : s * HQ + 8 * i + 8, :]
            pair = jnp.concatenate([jnp.where(upper, q, 0.0), jnp.where(upper, 0.0, q)], axis=1)
            parts.append(
                lax.dot_general(
                    pair.astype(jnp.bfloat16),
                    keys[s, :, 256 * i : 256 * i + 256],
                    (((1,), (1,)), ((), ())),
                    preferred_element_type=jnp.float32,
                )
            )
        full = jnp.concatenate(parts, axis=0) * HEAD_SIZE**-0.5
        scores.append(jnp.where(lane < lengths[pages[s]] - numbers[s] * PAGE, full, -1e30))
    scores = jnp.concatenate(scores, axis=0)
    top = jnp.max(scores, axis=1, keepdims=True)
    weights = jnp.exp(scores - top)
    total = jnp.sum(weights, axis=1, keepdims=True)
    rounded = weights.astype(jnp.bfloat16)
    outs = []
    for s in range(SLOTS):
        for i in range(4):
            both = jnp.dot(
                rounded[s * HQ + 8 * i : s * HQ + 8 * i + 8, :],
                values[s, :, 256 * i : 256 * i + 256],
                preferred_element_type=jnp.float32,
            )
            outs.append(jnp.where(upper, both[:, :128], both[:, 128:]))
    outs = jnp.concatenate(outs, axis=0) / total
    whole, stats = coded(outs, top + jnp.log(total))
    out[...] = jnp.zeros(out.shape, jnp.int16)
    for s in range(SLOTS):
        target = pages[s] // 8
        out[target, 0:HQ, :] = whole[s * HQ : s * HQ + HQ, :]
        turned = jnp.transpose(stats[s * HQ : s * HQ + HQ, :])
        tile = jnp.concatenate([turned[0:8, :], jnp.zeros((8, 96), jnp.float32)], axis=1)
        out[target, HQ:MESSAGE_ROWS, :] = tile.astype(jnp.int32).astype(jnp.int16)


def statistics(recv, count):
    tiles = recv[:, HQ:MESSAGE_ROWS, :].astype(jnp.int32).astype(jnp.float32)
    coarse, fine, power = tiles[:, 0, :], tiles[:, 1, :], tiles[:, 2, :]
    lse = coarse * 0.0625 + fine * (1.0 / 524288.0)
    return lse, jnp.exp2(power) * (1.0 / TOP)


def merge_kernel(recv, member, out):
    place = member[...]
    lse, unit = statistics(recv, 32)
    tops, sums = [], []
    peak = jnp.zeros((32, 128), jnp.float32)
    for j in range(8):
        top = jnp.max(jnp.where(place == j, lse, ABSENT), axis=0, keepdims=True)
        tops.append(top)
        peak = jnp.where(place == j, top, peak)
    weight = jnp.where(place >= 0.0, jnp.exp(lse - peak), 0.0)
    total = jnp.ones((32, 128), jnp.float32)
    for j in range(8):
        add = jnp.sum(jnp.where(place == j, weight, 0.0), axis=0, keepdims=True)
        sums.append(add)
        total = jnp.where(place == j, add, total)
    factor = jnp.transpose(weight / total * unit)[0:HQ, :]
    accs = [jnp.zeros((HQ, 128), jnp.float32) for _ in range(8)]
    for g in range(32):
        row = recv[g, 0:HQ, :].astype(jnp.int32).astype(jnp.float32)
        row = row * jnp.broadcast_to(factor[:, g : g + 1], (HQ, 128))
        at = jnp.broadcast_to(place[g : g + 1, :], (HQ, 128))
        accs = [acc + jnp.where(at == j, row, 0.0) for j, acc in enumerate(accs)]
    lses = [
        jnp.where(add > 0.0, top + jnp.log(jnp.maximum(add, 1e-30)), ABSENT)
        for top, add in zip(tops, sums)
    ]
    spare = jnp.zeros((8, 128), jnp.float32)
    for j in range(8):
        largest = jnp.max(jnp.abs(accs[j]), axis=1, keepdims=True)
        power = jnp.ceil(jnp.log2(jnp.maximum(largest, 1e-30)))
        whole = jnp.round(accs[j] * (jnp.exp2(-power) * TOP)).astype(jnp.int32)
        out[j, 0:HQ, :] = whole.astype(jnp.int16)
        coarse = jnp.round(lses[j] * 16.0)
        fine = jnp.round((lses[j] - coarse * 0.0625) * 524288.0)
        turned = jnp.transpose(jnp.broadcast_to(power, (HQ, 128)))[0:8, :]
        turned = jnp.concatenate([turned, jnp.zeros((8, 96), jnp.float32)], axis=1)
        row = iota((8, 128), 0)
        tile = jnp.where(row == 0, coarse, jnp.where(row == 1, fine, turned))
        tile = jnp.where(row < 3, tile, spare)
        out[j, HQ:MESSAGE_ROWS, :] = tile.astype(jnp.int32).astype(jnp.int16)


def finish_kernel(recv, out):
    lse, unit = statistics(recv, 8)
    top = jnp.max(lse, axis=0, keepdims=True)
    weight = jnp.exp(lse - top)
    total = jnp.sum(weight, axis=0, keepdims=True)
    factor = jnp.transpose(weight / total * unit)[0:HQ, :]
    acc = jnp.zeros((HQ, 128), jnp.float32)
    for k in range(8):
        row = recv[k, 0:HQ, :].astype(jnp.int32).astype(jnp.float32)
        acc = acc + row * jnp.broadcast_to(factor[:, k : k + 1], (HQ, 128))
    for h in range(HQ):
        out[0:1, 128 * h : 128 * h + 128] = acc[h : h + 1, :].astype(jnp.bfloat16)


VMEM = pl.BlockSpec(memory_space=pltpu.VMEM)
SMEM = pl.BlockSpec(memory_space=pltpu.SMEM)
HBM = pl.BlockSpec(memory_space=pltpu.MemorySpace.HBM)


def kernel_call(kernel, shapes, in_specs, name, out_specs=None, scratch=(), flops=None):
    return pl.pallas_call(
        kernel,
        out_shape=shapes,
        in_specs=in_specs,
        out_specs=jax.tree.map(lambda _: VMEM, shapes) if out_specs is None else out_specs,
        scratch_shapes=scratch,
        name=name,
        cost_estimate=flops and pl.CostEstimate(flops, 0, 0),
        compiler_params=pltpu.CompilerParams(vmem_limit_bytes=32 * 1024 * 1024),
    )


def on_device(queries, paged_key_cache, paged_value_cache, page_request, page_number, lengths):
    shape = jax.ShapeDtypeStruct
    sent = kernel_call(
        spread_kernel,
        shape((512, 128), jnp.bfloat16),
        [HBM, HBM],
        "spread",
        scratch=[
            pltpu.SMEM((SLOTS,), jnp.int32),
            pltpu.VMEM((1, HQ * HEAD_SIZE), jnp.bfloat16),
            pltpu.SemaphoreType.DMA((2,)),
        ],
    )(
        pltpu.with_memory_space_constraint(page_request, pltpu.MemorySpace.HBM),
        pltpu.with_memory_space_constraint(queries, pltpu.MemorySpace.HBM),
    )
    heads = lax.all_to_all(sent, ("req", "kv"), 0, 0, tiled=True)
    picked, member = kernel_call(
        select_kernel,
        (shape((256, 128), jnp.bfloat16), shape((32, 128), jnp.float32)),
        [VMEM],
        "select",
        flops=10**10,
    )(heads)
    wanted = lax.all_to_all(picked, "req", 0, 0, tiled=True)
    partial = kernel_call(
        attend_kernel,
        shape((32, MESSAGE_ROWS, 128), jnp.int16),
        [SMEM, SMEM, SMEM, VMEM, VMEM, VMEM],
        "attend",
    )(page_request, page_number, lengths, wanted, paged_key_cache, paged_value_cache)
    partial = lax.all_to_all(partial, "req", 0, 0, tiled=True)
    merged = kernel_call(
        merge_kernel, shape((8, MESSAGE_ROWS, 128), jnp.int16), [VMEM, VMEM], "merge"
    )(partial, member)
    merged = lax.all_to_all(merged, "kv", 0, 0, tiled=True)
    return kernel_call(finish_kernel, shape((1, 4096), jnp.bfloat16), [VMEM], "finish")(merged)


def solution(mesh):
    placed = (
        P(("req", "kv"), None),
        P(("req", "kv"), None, None),
        P(("req", "kv"), None, None),
        P(("req", "kv")),
        P(("req", "kv")),
        P(),
    )
    return jax.shard_map(
        on_device, mesh=mesh, in_specs=placed, out_specs=P(("req", "kv"), None), check_vma=False
    )
```

```python
import jax
import jax.numpy as jnp
from jax import lax
from jax.experimental import pallas as pl
from jax.experimental.pallas import tpu as pltpu
from jax.sharding import PartitionSpec as P

HQ = 32
HEAD_SIZE = 128
PAGE = 128
SLOTS = 6
SLOT_ROWS = 8
MESSAGE_ROWS = 40
ABSENT = -2048.0
TOP = 32767.0


def iota(shape, dim):
    return lax.broadcasted_iota(jnp.int32, shape, dim)


def spread_kernel(pages_in, query_in, out, pages, query, sems):
    first_copy = pltpu.make_async_copy(pages_in, pages, sems.at[0])
    second_copy = pltpu.make_async_copy(query_in, query, sems.at[1])
    first_copy.start()
    second_copy.start()
    first_copy.wait()
    second_copy.wait()
    lane = iota((16, 128), 1)
    even = iota((16, 128), 0) % 2 == 0
    first = (lax.axis_index("req") % 16) * SLOT_ROWS
    ids = jnp.zeros((16, 128), jnp.float32)
    for s in range(SLOTS):
        ids = jnp.where(lane == first + s, pages[s].astype(jnp.float32), ids)
    for h in range(HQ):
        head = query[0:1, h * 128 : (h + 1) * 128].astype(jnp.float32)
        block = jnp.where(even, jnp.broadcast_to(head, (16, 128)), ids)
        out[16 * h : 16 * h + 16, :] = block.astype(jnp.bfloat16)


def select_kernel(recv, out, member):
    rows = recv[...]
    group, plane = lax.axis_index("req"), lax.axis_index("kv")
    at, half = iota((8, 512), 1), iota((8, 512), 0)
    source = at // 2
    pick = (at % 2 == 1) & (source % 8 == plane) & (source // 128 == half)
    ids = jnp.dot(pick.astype(jnp.bfloat16), rows, preferred_element_type=jnp.float32)
    ids = ids.astype(jnp.int32)
    lane = iota((1, 128), 1)
    spots = []
    for n in range(2):
        wanted = ids[n : n + 1, :]
        hot = iota((512, 128), 0) == jnp.broadcast_to(2 * wanted, (512, 128))
        hot = hot.astype(jnp.float32).astype(jnp.bfloat16)
        got = lax.dot_general(
            hot, rows, (((0,), (0,)), ((), ())), preferred_element_type=jnp.float32
        )
        out[128 * n : 128 * n + 128, :] = got.astype(jnp.bfloat16)
        mine = (wanted // 8 == group) & (lane % 8 < SLOTS)
        spots.append(jnp.where(mine, wanted % 8 + 1, 0).astype(jnp.float32))
    dev, lanes = iota((32, 128), 0), iota((32, 128), 1)
    both = jnp.where(dev < 16, spots[0], spots[1])
    own = jnp.where(lanes // 8 == dev % 16, both, 0.0)
    place = jnp.sum(own, axis=1, keepdims=True) - 1.0
    member[...] = jnp.broadcast_to(place, (32, 128))


def attend_kernel(pages, numbers, lengths, recv, keys, values, out):
    whose, counts = pages[...], lengths[...].astype(jnp.float32)
    before = numbers[...].astype(jnp.float32) * PAGE
    request = iota(counts.shape, 1)
    limits, targets = [], []
    for s in range(SLOTS):
        own = request == whose[:, s : s + 1]
        count = jnp.sum(jnp.where(own, counts, 0.0), axis=1, keepdims=True)
        limits.append(jnp.broadcast_to(count - before[:, s : s + 1], (8, 128)))
        group = jnp.max(whose[:, s : s + 1].astype(jnp.float32)).astype(jnp.int32)
        targets.append(lax.shift_right_logical(group, 3))
    rows = SLOTS * HQ
    r, c = iota((rows, 256), 0), iota((rows, 256), 1)
    slot, head = r // 64 * 2 + r // 8 % 2, r // 16 % 4 * 8 + r % 8
    order = (c == head * SLOT_ROWS + slot).astype(jnp.float32).astype(jnp.bfloat16)
    query = jnp.dot(order, recv[...], preferred_element_type=jnp.float32)
    upper = iota((rows, 128), 0) % 8 < 4
    both = jnp.concatenate([jnp.where(upper, query, 0.0), jnp.where(upper, 0.0, query)], axis=1)
    both = both.astype(jnp.bfloat16)
    lane = iota((8, 128), 1).astype(jnp.float32)
    scores = []
    for p in range(SLOTS // 2):
        for i in range(4):
            at = 64 * p + 16 * i
            tile = lax.dot_general(
                both[at : at + 16, :],
                keys[2 * p : 2 * p + 2, :, 256 * i : 256 * i + 256].reshape(256, 256),
                (((1,), (1,)), ((), ())),
                preferred_element_type=jnp.float32,
            )
            for n in range(2):
                part = tile[8 * n : 8 * n + 8, 128 * n : 128 * n + 128] * HEAD_SIZE**-0.5
                scores.append(jnp.where(lane < limits[2 * p + n], part, -1e30))
    scores = jnp.concatenate(scores, axis=0)
    top = jnp.max(scores, axis=1, keepdims=True)
    weights = jnp.exp(scores - top)
    total = jnp.sum(weights, axis=1, keepdims=True)
    first = iota((rows, 128), 0) % 16 < 8
    wide = jnp.concatenate([jnp.where(first, weights, 0.0), jnp.where(first, 0.0, weights)], axis=1)
    wide = wide.astype(jnp.bfloat16)
    outs = []
    for p in range(SLOTS // 2):
        for i in range(4):
            at = 64 * p + 16 * i
            tile = jnp.dot(
                wide[at : at + 16, :],
                values[2 * p : 2 * p + 2, :, 256 * i : 256 * i + 256].reshape(256, 256),
                preferred_element_type=jnp.float32,
            )
            outs.append(jnp.where(upper[0:16, :], tile[:, :128], tile[:, 128:]))
    outs = jnp.concatenate(outs, axis=0) / total
    largest = jnp.max(jnp.abs(outs), axis=1, keepdims=True)
    power = jnp.ceil(jnp.log2(jnp.maximum(largest, 1e-30)))
    whole = jnp.round(outs * (jnp.exp2(-power) * TOP)).astype(jnp.int32).astype(jnp.int16)
    lanes = iota((rows, 128), 1)
    stats = jnp.where(lanes == 0, top + jnp.log(total), jnp.where(lanes == 1, power, 0.0))
    out[...] = jnp.zeros(out.shape, jnp.int16)
    for s in range(SLOTS):
        target = targets[s]
        starts = [64 * (s // 2) + 16 * i + 8 * (s % 2) for i in range(4)]
        out[target, 0:HQ, :] = jnp.concatenate([whole[a : a + 8, :] for a in starts], axis=0)
        turned = jnp.transpose(jnp.concatenate([stats[a : a + 8, :] for a in starts], axis=0))
        turned = jnp.concatenate([turned[0:8, :], jnp.zeros((8, 96), jnp.float32)], axis=1)
        out[target, HQ:MESSAGE_ROWS, :] = statistics_tile(turned[0:1, :], turned[1:2, :])


def statistics_tile(lse, power):
    row = iota((8, 128), 0)
    coarse = jnp.round(lse * 16.0)
    fine = jnp.round((lse - coarse * 0.0625) * 524288.0)
    tile = jnp.where(row == 0, coarse, jnp.where(row == 1, fine, jnp.where(row == 2, power, 0.0)))
    return tile.astype(jnp.int32).astype(jnp.int16)


def statistics(recv):
    tiles = recv[:, HQ:MESSAGE_ROWS, :].astype(jnp.int32).astype(jnp.float32)
    return tiles[:, 0, :] * 0.0625 + tiles[:, 1, :] * (1.0 / 524288.0), tiles[:, 2, :]


def merge_kernel(recv, member, out):
    place = member[...]
    lse, power = statistics(recv)
    peak, unit, total = (jnp.zeros((32, 128), jnp.float32) for _ in range(3))
    tops, units, sums = [], [], []
    for j in range(8):
        own = place == j
        tops.append(jnp.max(jnp.where(own, lse, ABSENT), axis=0, keepdims=True))
        units.append(jnp.max(jnp.where(own, power, -110.0), axis=0, keepdims=True))
        peak = jnp.where(own, tops[j], peak)
        unit = jnp.where(own, units[j], unit)
    weight = jnp.where(place >= 0.0, jnp.exp(lse - peak), 0.0)
    for j in range(8):
        own = place == j
        sums.append(jnp.sum(jnp.where(own, weight, 0.0), axis=0, keepdims=True))
        total = jnp.where(own, sums[j], total)
    total = jnp.where(place >= 0.0, total, 1.0)
    factor = jnp.transpose(weight / total * jnp.exp2(power - unit))[0:HQ, :]
    accs = [jnp.zeros((HQ, 128), jnp.float32) for _ in range(8)]
    for g in range(32):
        row = recv[g, 0:HQ, :].astype(jnp.int32).astype(jnp.float32)
        row = row * jnp.broadcast_to(factor[:, g : g + 1], (HQ, 128))
        at = jnp.broadcast_to(place[g : g + 1, :], (HQ, 128))
        accs = [acc + jnp.where(at == j, row, 0.0) for j, acc in enumerate(accs)]
    for j in range(8):
        out[j, 0:HQ, :] = jnp.round(accs[j]).astype(jnp.int32).astype(jnp.int16)
        lse = jnp.where(sums[j] > 0.0, tops[j] + jnp.log(jnp.maximum(sums[j], 1e-30)), ABSENT)
        out[j, HQ:MESSAGE_ROWS, :] = statistics_tile(lse, units[j])


def finish_kernel(recv, out):
    lse, power = statistics(recv)
    weight = jnp.exp(lse - jnp.max(lse, axis=0, keepdims=True))
    total = jnp.sum(weight, axis=0, keepdims=True)
    factor = jnp.transpose(weight / total * (jnp.exp2(power) * (1.0 / TOP)))[0:HQ, :]
    acc = jnp.zeros((HQ, 128), jnp.float32)
    for k in range(8):
        row = recv[k, 0:HQ, :].astype(jnp.int32).astype(jnp.float32)
        acc = acc + row * jnp.broadcast_to(factor[:, k : k + 1], (HQ, 128))
    for h in range(HQ):
        out[0:1, 128 * h : 128 * h + 128] = acc[h : h + 1, :].astype(jnp.bfloat16)


VMEM = pl.BlockSpec(memory_space=pltpu.VMEM)
HBM = pl.BlockSpec(memory_space=pltpu.MemorySpace.HBM)


def kernel_call(kernel, shapes, in_specs, name, scratch=(), flops=None):
    return pl.pallas_call(
        kernel,
        out_shape=shapes,
        in_specs=in_specs,
        out_specs=jax.tree.map(lambda _: VMEM, shapes),
        scratch_shapes=scratch,
        name=name,
        cost_estimate=flops and pl.CostEstimate(flops, 0, 0),
        compiler_params=pltpu.CompilerParams(vmem_limit_bytes=32 * 1024 * 1024),
    )


def on_device(queries, paged_key_cache, paged_value_cache, page_request, page_number, lengths):
    shape = jax.ShapeDtypeStruct
    sent = kernel_call(
        spread_kernel,
        shape((512, 128), jnp.bfloat16),
        [HBM, HBM],
        "spread",
        scratch=[
            pltpu.SMEM((SLOTS,), jnp.int32),
            pltpu.VMEM((1, HQ * HEAD_SIZE), jnp.bfloat16),
            pltpu.SemaphoreType.DMA((2,)),
        ],
    )(
        pltpu.with_memory_space_constraint(page_request, pltpu.MemorySpace.HBM),
        pltpu.with_memory_space_constraint(queries, pltpu.MemorySpace.HBM),
    )
    heads = lax.all_to_all(sent, ("req", "kv"), 0, 0, tiled=True)
    picked, member = kernel_call(
        select_kernel,
        (shape((256, 128), jnp.bfloat16), shape((32, 128), jnp.float32)),
        [VMEM],
        "select",
        flops=10**10,
    )(heads)
    wanted = lax.all_to_all(picked, "req", 0, 0, tiled=True)
    partial = kernel_call(
        attend_kernel,
        shape((32, MESSAGE_ROWS, 128), jnp.int16),
        [VMEM] * 6,
        "attend",
    )(
        page_request.reshape(1, -1),
        page_number.reshape(1, -1),
        lengths.reshape(1, -1),
        wanted,
        paged_key_cache,
        paged_value_cache,
    )
    partial = lax.all_to_all(partial, "req", 0, 0, tiled=True)
    merged = kernel_call(
        merge_kernel, shape((8, MESSAGE_ROWS, 128), jnp.int16), [VMEM, VMEM], "merge"
    )(partial, member)
    merged = lax.all_to_all(merged, "kv", 0, 0, tiled=True)
    return kernel_call(finish_kernel, shape((1, 4096), jnp.bfloat16), [VMEM], "finish")(merged)


def solution(mesh):
    placed = (
        P(("req", "kv"), None),
        P(("req", "kv"), None, None),
        P(("req", "kv"), None, None),
        P(("req", "kv")),
        P(("req", "kv")),
        P(),
    )
    return jax.shard_map(
        on_device, mesh=mesh, in_specs=placed, out_specs=P(("req", "kv"), None), check_vma=False
    )
```

```python
import jax
import jax.numpy as jnp
from jax import lax
from jax.experimental import pallas as pl
from jax.experimental.pallas import tpu as pltpu
from jax.sharding import PartitionSpec as P

HQ = 32
HEAD_SIZE = 128
PAGE = 128
SLOTS = 6
SLOT_ROWS = 8
MESSAGE_ROWS = 40
ABSENT = -2048.0
TOP = 32767.0


def iota(shape, dim):
    return lax.broadcasted_iota(jnp.int32, shape, dim)


def spread_kernel(pages_in, query_in, out, pages, query, sems):
    first_copy = pltpu.make_async_copy(pages_in, pages, sems.at[0])
    second_copy = pltpu.make_async_copy(query_in, query, sems.at[1])
    first_copy.start()
    second_copy.start()
    first_copy.wait()
    lane = iota((16, 128), 1)
    even = iota((16, 128), 0) % 2 == 0
    first = (lax.axis_index("req") % 16) * SLOT_ROWS
    ids = jnp.zeros((16, 128), jnp.float32)
    for s in range(SLOTS):
        ids = jnp.where(lane == first + s, pages[s].astype(jnp.float32), ids)
    second_copy.wait()
    for h in range(HQ):
        head = query[0:1, h * 128 : (h + 1) * 128].astype(jnp.float32)
        block = jnp.where(even, jnp.broadcast_to(head, (16, 128)), ids)
        out[16 * h : 16 * h + 16, :] = block.astype(jnp.bfloat16)


def select_kernel(recv, out, member):
    rows = recv[...]
    group, plane = lax.axis_index("req"), lax.axis_index("kv")
    at, half = iota((8, 512), 1), iota((8, 512), 0)
    source = at // 2
    pick = (at % 2 == 1) & (source % 8 == plane) & (source // 128 == half)
    ids = jnp.dot(pick.astype(jnp.bfloat16), rows, preferred_element_type=jnp.float32)
    ids = ids.astype(jnp.int32)
    lane = iota((1, 128), 1)
    spots = []
    for n in range(2):
        wanted = ids[n : n + 1, :]
        hot = iota((512, 128), 0) == jnp.broadcast_to(2 * wanted, (512, 128))
        hot = hot.astype(jnp.float32).astype(jnp.bfloat16)
        got = lax.dot_general(
            hot, rows, (((0,), (0,)), ((), ())), preferred_element_type=jnp.float32
        )
        out[128 * n : 128 * n + 128, :] = got.astype(jnp.bfloat16)
        mine = (wanted // 8 == group) & (lane % 8 < SLOTS)
        spots.append(jnp.where(mine, wanted % 8 + 1, 0).astype(jnp.float32))
    dev, lanes = iota((32, 128), 0), iota((32, 128), 1)
    both = jnp.where(dev < 16, spots[0], spots[1])
    own = jnp.where(lanes // 8 == dev % 16, both, 0.0)
    place = jnp.sum(own, axis=1, keepdims=True) - 1.0
    member[...] = jnp.broadcast_to(place, (32, 128))


def attend_kernel(pages, numbers, lengths, recv, keys, values, out):
    whose, counts = pages[...], lengths[...].astype(jnp.float32)
    before = numbers[...].astype(jnp.float32) * PAGE
    request = iota(counts.shape, 1)
    limits, targets = [], []
    for s in range(SLOTS):
        own = request == whose[:, s : s + 1]
        count = jnp.sum(jnp.where(own, counts, 0.0), axis=1, keepdims=True)
        limits.append(jnp.broadcast_to(count - before[:, s : s + 1], (8, 128)))
        group = jnp.max(whose[:, s : s + 1].astype(jnp.float32)).astype(jnp.int32)
        targets.append(lax.shift_right_logical(group, 3))
    rows = SLOTS * HQ
    r, c = iota((rows, 256), 0), iota((rows, 256), 1)
    slot, head = r // 64 * 2 + r // 8 % 2, r // 16 % 4 * 8 + r % 8
    order = (c == head * SLOT_ROWS + slot).astype(jnp.float32).astype(jnp.bfloat16)
    query = jnp.dot(order, recv[...], preferred_element_type=jnp.float32)
    upper = iota((rows, 128), 0) % 8 < 4
    both = jnp.concatenate([jnp.where(upper, query, 0.0), jnp.where(upper, 0.0, query)], axis=1)
    both = both.astype(jnp.bfloat16)
    lane = iota((8, 128), 1).astype(jnp.float32)
    scores = []
    for p in range(SLOTS // 2):
        for i in range(4):
            at = 64 * p + 16 * i
            tile = lax.dot_general(
                both[at : at + 16, :],
                keys[2 * p : 2 * p + 2, :, 256 * i : 256 * i + 256].reshape(256, 256),
                (((1,), (1,)), ((), ())),
                preferred_element_type=jnp.float32,
            )
            for n in range(2):
                part = tile[8 * n : 8 * n + 8, 128 * n : 128 * n + 128] * HEAD_SIZE**-0.5
                scores.append(jnp.where(lane < limits[2 * p + n], part, -1e30))
    scores = jnp.concatenate(scores, axis=0)
    top = jnp.max(scores, axis=1, keepdims=True)
    weights = jnp.exp(scores - top)
    total = jnp.sum(weights, axis=1, keepdims=True)
    first = iota((rows, 128), 0) % 16 < 8
    wide = jnp.concatenate([jnp.where(first, weights, 0.0), jnp.where(first, 0.0, weights)], axis=1)
    wide = wide.astype(jnp.bfloat16)
    outs = []
    for p in range(SLOTS // 2):
        for i in range(4):
            at = 64 * p + 16 * i
            tile = jnp.dot(
                wide[at : at + 16, :],
                values[2 * p : 2 * p + 2, :, 256 * i : 256 * i + 256].reshape(256, 256),
                preferred_element_type=jnp.float32,
            )
            outs.append(jnp.where(upper[0:16, :], tile[:, :128], tile[:, 128:]))
    outs = jnp.concatenate(outs, axis=0) / total
    largest = jnp.max(jnp.abs(outs), axis=1, keepdims=True)
    power = jnp.ceil(jnp.log2(jnp.maximum(largest, 1e-30)))
    whole = jnp.round(outs * (jnp.exp2(-power) * TOP)).astype(jnp.int32).astype(jnp.int16)
    lanes = iota((rows, 128), 1)
    stats = jnp.where(lanes == 0, top + jnp.log(total), jnp.where(lanes == 1, power, 0.0))
    out[...] = jnp.zeros(out.shape, jnp.int16)
    for s in range(SLOTS):
        target = targets[s]
        starts = [64 * (s // 2) + 16 * i + 8 * (s % 2) for i in range(4)]
        out[target, 0:HQ, :] = jnp.concatenate([whole[a : a + 8, :] for a in starts], axis=0)
        turned = jnp.transpose(jnp.concatenate([stats[a : a + 8, :] for a in starts], axis=0))
        turned = jnp.concatenate([turned[0:8, :], jnp.zeros((8, 96), jnp.float32)], axis=1)
        out[target, HQ:MESSAGE_ROWS, :] = statistics_tile(turned[0:1, :], turned[1:2, :])


def statistics_tile(lse, power):
    row = iota((8, 128), 0)
    coarse = jnp.round(lse * 16.0)
    fine = jnp.round((lse - coarse * 0.0625) * 524288.0)
    tile = jnp.where(row == 0, coarse, jnp.where(row == 1, fine, jnp.where(row == 2, power, 0.0)))
    return tile.astype(jnp.int32).astype(jnp.int16)


def statistics(recv):
    tiles = recv[:, HQ:MESSAGE_ROWS, :].astype(jnp.int32).astype(jnp.float32)
    return tiles[:, 0, :] * 0.0625 + tiles[:, 1, :] * (1.0 / 524288.0), tiles[:, 2, :]


def merge_kernel(recv, member, out, sums_of):
    place = member[...]
    lse, power = statistics(recv)
    peak, unit, total = (jnp.zeros((32, 128), jnp.float32) for _ in range(3))
    tops, units, sums = [], [], []
    for j in range(8):
        own = place == j
        tops.append(jnp.max(jnp.where(own, lse, ABSENT), axis=0, keepdims=True))
        units.append(jnp.max(jnp.where(own, power, -110.0), axis=0, keepdims=True))
        peak = jnp.where(own, tops[j], peak)
        unit = jnp.where(own, units[j], unit)
    weight = jnp.where(place >= 0.0, jnp.exp(lse - peak), 0.0)
    for j in range(8):
        own = place == j
        sums.append(jnp.sum(jnp.where(own, weight, 0.0), axis=0, keepdims=True))
        total = jnp.where(own, sums[j], total)
    total = jnp.where(place >= 0.0, total, 1.0)
    factor = jnp.transpose(weight / total * jnp.exp2(power - unit))[0:HQ, :]
    sums_of[...] = jnp.zeros(sums_of.shape, jnp.float32)
    for g in range(32):
        row = recv[g, 0:HQ, :].astype(jnp.int32).astype(jnp.float32)
        row = row * jnp.broadcast_to(factor[:, g : g + 1], (HQ, 128))
        j = jnp.max(place[g : g + 1, 0:1]).astype(jnp.int32)
        j = jnp.where(j < 0, 8, j)
        sums_of[j + 9 * (g % 2)] = sums_of[j + 9 * (g % 2)] + row
    for j in range(8):
        out[j, 0:HQ, :] = jnp.round(sums_of[j] + sums_of[j + 9]).astype(jnp.int32).astype(jnp.int16)
        lse = jnp.where(sums[j] > 0.0, tops[j] + jnp.log(jnp.maximum(sums[j], 1e-30)), ABSENT)
        out[j, HQ:MESSAGE_ROWS, :] = statistics_tile(lse, units[j])


def finish_kernel(recv, out):
    lse, power = statistics(recv)
    weight = jnp.exp(lse - jnp.max(lse, axis=0, keepdims=True))
    total = jnp.sum(weight, axis=0, keepdims=True)
    factor = jnp.transpose(weight / total * (jnp.exp2(power) * (1.0 / TOP)))[0:HQ, :]
    acc = jnp.zeros((HQ, 128), jnp.float32)
    for k in range(8):
        row = recv[k, 0:HQ, :].astype(jnp.int32).astype(jnp.float32)
        acc = acc + row * jnp.broadcast_to(factor[:, k : k + 1], (HQ, 128))
    for h in range(HQ):
        out[0:1, 128 * h : 128 * h + 128] = acc[h : h + 1, :].astype(jnp.bfloat16)


VMEM = pl.BlockSpec(memory_space=pltpu.VMEM)
HBM = pl.BlockSpec(memory_space=pltpu.MemorySpace.HBM)


def kernel_call(kernel, shapes, in_specs, name, scratch=(), flops=None):
    return pl.pallas_call(
        kernel,
        out_shape=shapes,
        in_specs=in_specs,
        out_specs=jax.tree.map(lambda _: VMEM, shapes),
        scratch_shapes=scratch,
        name=name,
        cost_estimate=flops and pl.CostEstimate(flops, 0, 0),
        compiler_params=pltpu.CompilerParams(vmem_limit_bytes=32 * 1024 * 1024),
    )


def on_device(queries, paged_key_cache, paged_value_cache, page_request, page_number, lengths):
    shape = jax.ShapeDtypeStruct
    sent = kernel_call(
        spread_kernel,
        shape((512, 128), jnp.bfloat16),
        [HBM, HBM],
        "spread",
        scratch=[
            pltpu.SMEM((SLOTS,), jnp.int32),
            pltpu.VMEM((1, HQ * HEAD_SIZE), jnp.bfloat16),
            pltpu.SemaphoreType.DMA((2,)),
        ],
    )(
        pltpu.with_memory_space_constraint(page_request, pltpu.MemorySpace.HBM),
        pltpu.with_memory_space_constraint(queries, pltpu.MemorySpace.HBM),
    )
    heads = lax.all_to_all(sent, ("req", "kv"), 0, 0, tiled=True)
    picked, member = kernel_call(
        select_kernel,
        (shape((256, 128), jnp.bfloat16), shape((32, 128), jnp.float32)),
        [VMEM],
        "select",
        flops=10**10,
    )(heads)
    wanted = lax.all_to_all(picked, "req", 0, 0, tiled=True)
    partial = kernel_call(
        attend_kernel,
        shape((32, MESSAGE_ROWS, 128), jnp.int16),
        [VMEM] * 6,
        "attend",
    )(
        page_request.reshape(1, -1),
        page_number.reshape(1, -1),
        lengths.reshape(1, -1),
        wanted,
        paged_key_cache,
        paged_value_cache,
    )
    partial = lax.all_to_all(partial, "req", 0, 0, tiled=True)
    merged = kernel_call(
        merge_kernel,
        shape((8, MESSAGE_ROWS, 128), jnp.int16),
        [VMEM, VMEM],
        "merge",
        [pltpu.VMEM((18, HQ, 128), jnp.float32)],
    )(partial, member)
    merged = lax.all_to_all(merged, "kv", 0, 0, tiled=True)
    return kernel_call(finish_kernel, shape((1, 4096), jnp.bfloat16), [VMEM], "finish")(merged)


def solution(mesh):
    placed = (
        P(("req", "kv"), None),
        P(("req", "kv"), None, None),
        P(("req", "kv"), None, None),
        P(("req", "kv")),
        P(("req", "kv")),
        P(),
    )
    return jax.shard_map(
        on_device, mesh=mesh, in_specs=placed, out_specs=P(("req", "kv"), None), check_vma=False
    )
```

```python
import jax
import jax.numpy as jnp
from jax import lax
from jax.experimental import pallas as pl
from jax.experimental.pallas import tpu as pltpu
from jax.sharding import PartitionSpec as P

HQ = 32
HEAD_SIZE = 128
PAGE = 128
SLOTS = 6
SLOT_ROWS = 8
MESSAGE_ROWS = 40
SHORT_ROWS = 34
ABSENT = -2048.0
TOP = 32767.0


def iota(shape, dim):
    return lax.broadcasted_iota(jnp.int32, shape, dim)


def spread_kernel(pages_in, query_in, out, pages, query, sems):
    first_copy = pltpu.make_async_copy(pages_in, pages, sems.at[0])
    second_copy = pltpu.make_async_copy(query_in, query, sems.at[1])
    first_copy.start()
    second_copy.start()
    first_copy.wait()
    lane = iota((16, 128), 1)
    even = iota((16, 128), 0) % 2 == 0
    first = (lax.axis_index("req") % 16) * SLOT_ROWS
    ids = jnp.zeros((16, 128), jnp.float32)
    for s in range(SLOTS):
        ids = jnp.where(lane == first + s, pages[s].astype(jnp.float32), ids)
    second_copy.wait()
    for h in range(HQ):
        head = query[0:1, h * 128 : (h + 1) * 128].astype(jnp.float32)
        block = jnp.where(even, jnp.broadcast_to(head, (16, 128)), ids)
        out[16 * h : 16 * h + 16, :] = block.astype(jnp.bfloat16)


def select_kernel(recv, out, member):
    rows = recv[...]
    group, plane = lax.axis_index("req"), lax.axis_index("kv")
    at, half = iota((8, 512), 1), iota((8, 512), 0)
    source = at // 2
    pick = (at % 2 == 1) & (source % 8 == plane) & (source // 128 == half)
    ids = jnp.dot(pick.astype(jnp.bfloat16), rows, preferred_element_type=jnp.float32)
    ids = ids.astype(jnp.int32)
    lane = iota((1, 128), 1)
    spots = []
    for n in range(2):
        wanted = ids[n : n + 1, :]
        hot = iota((512, 128), 0) == jnp.broadcast_to(2 * wanted, (512, 128))
        hot = hot.astype(jnp.float32).astype(jnp.bfloat16)
        got = lax.dot_general(
            hot, rows, (((0,), (0,)), ((), ())), preferred_element_type=jnp.float32
        )
        out[128 * n : 128 * n + 128, :] = got.astype(jnp.bfloat16)
        mine = (wanted // 8 == group) & (lane % 8 < SLOTS)
        spots.append(jnp.where(mine, wanted % 8 + 1, 0).astype(jnp.float32))
    dev, lanes = iota((32, 128), 0), iota((32, 128), 1)
    both = jnp.where(dev < 16, spots[0], spots[1])
    own = jnp.where(lanes // 8 == dev % 16, both, 0.0)
    place = jnp.sum(own, axis=1, keepdims=True) - 1.0
    member[...] = jnp.broadcast_to(place, (32, 128))


def attend_kernel(pages, numbers, lengths, recv, keys, values, out):
    whose, counts = pages[...], lengths[...].astype(jnp.float32)
    before = numbers[...].astype(jnp.float32) * PAGE
    request = iota(counts.shape, 1)
    limits, targets = [], []
    for s in range(SLOTS):
        own = request == whose[:, s : s + 1]
        count = jnp.sum(jnp.where(own, counts, 0.0), axis=1, keepdims=True)
        limits.append(jnp.broadcast_to(count - before[:, s : s + 1], (8, 128)))
        group = jnp.max(whose[:, s : s + 1].astype(jnp.float32)).astype(jnp.int32)
        targets.append(lax.shift_right_logical(group, 3))
    rows = SLOTS * HQ
    r, c = iota((rows, 256), 0), iota((rows, 256), 1)
    slot, head = r // 64 * 2 + r // 8 % 2, r // 16 % 4 * 8 + r % 8
    order = (c == head * SLOT_ROWS + slot).astype(jnp.float32).astype(jnp.bfloat16)
    query = jnp.dot(order, recv[...], preferred_element_type=jnp.float32)
    upper = iota((64, 128), 0) % 8 < 4
    first = iota((64, 128), 0) % 16 < 8
    lane = iota((8, 128), 1).astype(jnp.float32)
    lanes = iota((64, 128), 1)

    def score(p):
        rows = query[64 * p : 64 * p + 64, :]
        both = jnp.concatenate([jnp.where(upper, rows, 0.0), jnp.where(upper, 0.0, rows)], axis=1)
        both = both.astype(jnp.bfloat16)
        scores = []
        for i in range(4):
            tile = lax.dot_general(
                both[16 * i : 16 * i + 16, :],
                keys[2 * p : 2 * p + 2, :, 256 * i : 256 * i + 256].reshape(256, 256),
                (((1,), (1,)), ((), ())),
                preferred_element_type=jnp.float32,
            )
            for n in range(2):
                part = tile[8 * n : 8 * n + 8, 128 * n : 128 * n + 128] * HEAD_SIZE**-0.5
                scores.append(jnp.where(lane < limits[2 * p + n], part, -1e30))
        return jnp.concatenate(scores, axis=0)

    def weigh(scores):
        top = jnp.max(scores, axis=1, keepdims=True)
        weights = jnp.exp(scores - top)
        total = jnp.sum(weights, axis=1, keepdims=True)
        wide = [jnp.where(first, weights, 0.0), jnp.where(first, 0.0, weights)]
        return jnp.concatenate(wide, axis=1).astype(jnp.bfloat16), top, total

    def add_up(p, wide):
        outs = []
        for i in range(4):
            tile = jnp.dot(
                wide[16 * i : 16 * i + 16, :],
                values[2 * p : 2 * p + 2, :, 256 * i : 256 * i + 256].reshape(256, 256),
                preferred_element_type=jnp.float32,
            )
            outs.append(jnp.where(upper[0:16, :], tile[:, :128], tile[:, 128:]))
        return jnp.concatenate(outs, axis=0)

    def send(p, outs, top, total):
        outs = outs / total
        largest = jnp.max(jnp.abs(outs), axis=1, keepdims=True)
        power = jnp.ceil(jnp.log2(jnp.maximum(largest, 1e-30)))
        whole = jnp.round(outs * (jnp.exp2(-power) * TOP))
        stats = jnp.where(lanes == 0, top + jnp.log(total), jnp.where(lanes == 1, power, 0.0))
        for n in range(2):
            target = targets[2 * p + n]
            starts = [16 * i + 8 * n for i in range(4)]
            turned = jnp.transpose(jnp.concatenate([stats[a : a + 8, :] for a in starts], axis=0))
            line = statistics_row(turned[0:1, :], turned[1:2, :])
            block = jnp.concatenate([whole[a : a + 8, :] for a in starts] + [line], axis=0)
            past = target * SHORT_ROWS % 8
            block = pltpu.roll(block, past, 0).astype(jnp.int32)
            at = pl.ds(pl.multiple_of(target * SHORT_ROWS - past, 8), MESSAGE_ROWS)
            out[at, :] = (out[at, :].astype(jnp.int32) + block).astype(jnp.int16)

    out[...] = jnp.zeros(out.shape, jnp.int16)
    scores = [score(0), score(1)]
    soft = [weigh(scores[0])]
    scores.append(score(2))
    sums = [add_up(0, soft[0][0])]
    soft.append(weigh(scores[1]))
    sums.append(add_up(1, soft[1][0]))
    soft.append(weigh(scores[2]))
    send(0, sums[0], *soft[0][1:])
    sums.append(add_up(2, soft[2][0]))
    send(1, sums[1], *soft[1][1:])
    send(2, sums[2], *soft[2][1:])


def statistics_row(lse, power):
    coarse = jnp.round(lse * 16.0)
    fine = jnp.round((lse - coarse * 0.0625) * 524288.0)
    line = jnp.concatenate([coarse, fine, power, jnp.zeros((1, 32), jnp.float32)], axis=1)
    return jnp.where(iota((8, 128), 0) == 0, jnp.broadcast_to(line, (8, 128)), 0.0)


def statistics_tile(lse, power):
    row = iota((8, 128), 0)
    coarse = jnp.round(lse * 16.0)
    fine = jnp.round((lse - coarse * 0.0625) * 524288.0)
    tile = jnp.where(row == 0, coarse, jnp.where(row == 1, fine, jnp.where(row == 2, power, 0.0)))
    return tile.astype(jnp.int32).astype(jnp.int16)


def statistics(recv):
    tiles = recv[:, HQ:MESSAGE_ROWS, :].astype(jnp.int32).astype(jnp.float32)
    return tiles[:, 0, :] * 0.0625 + tiles[:, 1, :] * (1.0 / 524288.0), tiles[:, 2, :]


def merge_kernel(recv, member, out, sums_of):
    place = member[...]
    lines = [
        recv[SHORT_ROWS * g + HQ : SHORT_ROWS * (g + 1), :].astype(jnp.int32).astype(jnp.float32)[0:1]
        for g in range(32)
    ]
    tile = jnp.concatenate(lines, axis=0)
    lse = tile * 0.0625 + pltpu.roll(tile, 96, 1) * (1.0 / 524288.0)
    power = pltpu.roll(tile, 64, 1)
    peak, unit, total = (jnp.zeros((32, 128), jnp.float32) for _ in range(3))
    tops, units, sums = [], [], []
    for j in range(8):
        own = place == j
        tops.append(jnp.max(jnp.where(own, lse, ABSENT), axis=0, keepdims=True))
        units.append(jnp.max(jnp.where(own, power, -110.0), axis=0, keepdims=True))
        peak = jnp.where(own, tops[j], peak)
        unit = jnp.where(own, units[j], unit)
    weight = jnp.where(place >= 0.0, jnp.exp(lse - peak), 0.0)
    for j in range(8):
        own = place == j
        sums.append(jnp.sum(jnp.where(own, weight, 0.0), axis=0, keepdims=True))
        total = jnp.where(own, sums[j], total)
    total = jnp.where(place >= 0.0, total, 1.0)
    factor = jnp.transpose(weight / total * jnp.exp2(power - unit))[0:HQ, :]
    sums_of[...] = jnp.zeros(sums_of.shape, jnp.float32)
    for g in range(32):
        row = recv[SHORT_ROWS * g : SHORT_ROWS * g + HQ, :].astype(jnp.int32).astype(jnp.float32)
        row = row * jnp.broadcast_to(factor[:, g : g + 1], (HQ, 128))
        j = jnp.max(place[g : g + 1, 0:1]).astype(jnp.int32)
        j = jnp.where(j < 0, 8, j)
        sums_of[j + 9 * (g % 2)] = sums_of[j + 9 * (g % 2)] + row
    for j in range(8):
        out[j, 0:HQ, :] = jnp.round(sums_of[j] + sums_of[j + 9]).astype(jnp.int32).astype(jnp.int16)
        lse = jnp.where(sums[j] > 0.0, tops[j] + jnp.log(jnp.maximum(sums[j], 1e-30)), ABSENT)
        out[j, HQ:MESSAGE_ROWS, :] = statistics_tile(lse, units[j])


def finish_kernel(recv, out):
    lse, power = statistics(recv)
    weight = jnp.exp(lse - jnp.max(lse, axis=0, keepdims=True))
    total = jnp.sum(weight, axis=0, keepdims=True)
    factor = jnp.transpose(weight / total * (jnp.exp2(power) * (1.0 / TOP)))[0:HQ, :]
    acc = jnp.zeros((HQ, 128), jnp.float32)
    for k in range(8):
        row = recv[k, 0:HQ, :].astype(jnp.int32).astype(jnp.float32)
        acc = acc + row * jnp.broadcast_to(factor[:, k : k + 1], (HQ, 128))
    for h in range(HQ):
        out[0:1, 128 * h : 128 * h + 128] = acc[h : h + 1, :].astype(jnp.bfloat16)


VMEM = pl.BlockSpec(memory_space=pltpu.VMEM)
HBM = pl.BlockSpec(memory_space=pltpu.MemorySpace.HBM)


def kernel_call(kernel, shapes, in_specs, name, scratch=(), flops=None):
    return pl.pallas_call(
        kernel,
        out_shape=shapes,
        in_specs=in_specs,
        out_specs=jax.tree.map(lambda _: VMEM, shapes),
        scratch_shapes=scratch,
        name=name,
        cost_estimate=flops and pl.CostEstimate(flops, 0, 0),
        compiler_params=pltpu.CompilerParams(vmem_limit_bytes=32 * 1024 * 1024),
    )


def on_device(queries, paged_key_cache, paged_value_cache, page_request, page_number, lengths):
    shape = jax.ShapeDtypeStruct
    sent = kernel_call(
        spread_kernel,
        shape((512, 128), jnp.bfloat16),
        [HBM, HBM],
        "spread",
        scratch=[
            pltpu.SMEM((SLOTS,), jnp.int32),
            pltpu.VMEM((1, HQ * HEAD_SIZE), jnp.bfloat16),
            pltpu.SemaphoreType.DMA((2,)),
        ],
    )(
        pltpu.with_memory_space_constraint(page_request, pltpu.MemorySpace.HBM),
        pltpu.with_memory_space_constraint(queries, pltpu.MemorySpace.HBM),
    )
    heads = lax.all_to_all(sent, ("req", "kv"), 0, 0, tiled=True)
    picked, member = kernel_call(
        select_kernel,
        (shape((256, 128), jnp.bfloat16), shape((32, 128), jnp.float32)),
        [VMEM],
        "select",
        flops=10**10,
    )(heads)
    wanted = lax.all_to_all(picked, "req", 0, 0, tiled=True)
    partial = kernel_call(
        attend_kernel,
        shape((32 * SHORT_ROWS, 128), jnp.int16),
        [VMEM] * 6,
        "attend",
    )(
        page_request.reshape(1, -1),
        page_number.reshape(1, -1),
        lengths.reshape(1, -1),
        wanted,
        paged_key_cache,
        paged_value_cache,
    )
    partial = partial.reshape(32, SHORT_ROWS // 2, 2, 128)
    partial = lax.all_to_all(partial, "req", 0, 0, tiled=True).reshape(32 * SHORT_ROWS, 128)
    merged = kernel_call(
        merge_kernel,
        shape((8, MESSAGE_ROWS, 128), jnp.int16),
        [VMEM, VMEM],
        "merge",
        [pltpu.VMEM((18, HQ, 128), jnp.float32)],
    )(partial, member)
    merged = lax.all_to_all(merged, "kv", 0, 0, tiled=True)
    return kernel_call(finish_kernel, shape((1, 4096), jnp.bfloat16), [VMEM], "finish")(merged)


def solution(mesh):
    placed = (
        P(("req", "kv"), None),
        P(("req", "kv"), None, None),
        P(("req", "kv"), None, None),
        P(("req", "kv")),
        P(("req", "kv")),
        P(),
    )
    return jax.shard_map(
        on_device, mesh=mesh, in_specs=placed, out_specs=P(("req", "kv"), None), check_vma=False
    )
```

```python
import jax
import jax.numpy as jnp
from jax import lax
from jax.experimental import pallas as pl
from jax.experimental.pallas import tpu as pltpu
from jax.sharding import PartitionSpec as P

HQ = 32
HEAD_SIZE = 128
PAGE = 128
SLOTS = 6
SLOT_ROWS = 8
MESSAGE_ROWS = 40
SHORT_ROWS = 34
ABSENT = -2048.0
TOP = 32767.0


def iota(shape, dim):
    return lax.broadcasted_iota(jnp.int32, shape, dim)


def spread_kernel(pages_in, query_in, out, pages, query, sems):
    first_copy = pltpu.make_async_copy(pages_in, pages, sems.at[0])
    second_copy = pltpu.make_async_copy(query_in, query, sems.at[1])
    first_copy.start()
    second_copy.start()
    first_copy.wait()
    lane = iota((16, 128), 1)
    even = iota((16, 128), 0) % 2 == 0
    first = (lax.axis_index("req") % 16) * SLOT_ROWS
    ids = jnp.zeros((16, 128), jnp.float32)
    for s in range(SLOTS):
        ids = jnp.where(lane == first + s, pages[s].astype(jnp.float32), ids)
    second_copy.wait()
    for h in range(HQ):
        head = query[0:1, h * 128 : (h + 1) * 128].astype(jnp.float32)
        block = jnp.where(even, jnp.broadcast_to(head, (16, 128)), ids)
        out[16 * h : 16 * h + 16, :] = block.astype(jnp.bfloat16)


def select_kernel(recv, out, member):
    rows = recv[...]
    group, plane = lax.axis_index("req"), lax.axis_index("kv")
    at, half = iota((8, 512), 1), iota((8, 512), 0)
    source = at // 2
    pick = (at % 2 == 1) & (source % 8 == plane) & (source // 128 == half)
    ids = jnp.dot(pick.astype(jnp.bfloat16), rows, preferred_element_type=jnp.float32)
    ids = ids.astype(jnp.int32)
    lane = iota((1, 128), 1)
    spots = []
    for n in range(2):
        wanted = ids[n : n + 1, :]
        hot = iota((512, 128), 0) == jnp.broadcast_to(2 * wanted, (512, 128))
        hot = hot.astype(jnp.float32).astype(jnp.bfloat16)
        got = lax.dot_general(
            hot, rows, (((0,), (0,)), ((), ())), preferred_element_type=jnp.float32
        )
        out[128 * n : 128 * n + 128, :] = got.astype(jnp.bfloat16)
        mine = (wanted // 8 == group) & (lane % 8 < SLOTS)
        spots.append(jnp.where(mine, wanted % 8 + 1, 0).astype(jnp.float32))
    dev, lanes = iota((32, 128), 0), iota((32, 128), 1)
    both = jnp.where(dev < 16, spots[0], spots[1])
    own = jnp.where(lanes // 8 == dev % 16, both, 0.0)
    place = jnp.sum(own, axis=1, keepdims=True) - 1.0
    member[...] = jnp.broadcast_to(place, (32, 128))


def attend_kernel(pages, numbers, lengths, recv, keys, values, out):
    whose, counts = pages[...], lengths[...].astype(jnp.float32)
    before = numbers[...].astype(jnp.float32) * PAGE
    request = iota(counts.shape, 1)
    limits, targets = [], []
    for s in range(SLOTS):
        own = request == whose[:, s : s + 1]
        count = jnp.sum(jnp.where(own, counts, 0.0), axis=1, keepdims=True)
        limits.append(jnp.broadcast_to(count - before[:, s : s + 1], (8, 128)))
        group = jnp.max(whose[:, s : s + 1].astype(jnp.float32)).astype(jnp.int32)
        targets.append(lax.shift_right_logical(group, 3))
    rows = SLOTS * HQ
    r, c = iota((rows, 256), 0), iota((rows, 256), 1)
    slot, head = r // 64 * 2 + r // 8 % 2, r // 16 % 4 * 8 + r % 8
    order = (c == head * SLOT_ROWS + slot).astype(jnp.float32).astype(jnp.bfloat16)
    query = jnp.dot(order, recv[...], preferred_element_type=jnp.float32)
    upper = iota((64, 128), 0) % 8 < 4
    first = iota((64, 128), 0) % 16 < 8
    lane = iota((8, 128), 1).astype(jnp.float32)
    lanes = iota((64, 128), 1)

    def score(p):
        rows = query[64 * p : 64 * p + 64, :]
        both = jnp.concatenate([jnp.where(upper, rows, 0.0), jnp.where(upper, 0.0, rows)], axis=1)
        both = both.astype(jnp.bfloat16)
        scores = []
        for i in range(4):
            tile = lax.dot_general(
                both[16 * i : 16 * i + 16, :],
                keys[2 * p : 2 * p + 2, :, 256 * i : 256 * i + 256].reshape(256, 256),
                (((1,), (1,)), ((), ())),
                preferred_element_type=jnp.float32,
            )
            for n in range(2):
                part = tile[8 * n : 8 * n + 8, 128 * n : 128 * n + 128] * HEAD_SIZE**-0.5
                scores.append(jnp.where(lane < limits[2 * p + n], part, -1e30))
        return jnp.concatenate(scores, axis=0)

    def weigh(scores):
        top = jnp.max(scores, axis=1, keepdims=True)
        weights = jnp.exp(scores - top)
        total = jnp.sum(weights, axis=1, keepdims=True)
        wide = [jnp.where(first, weights, 0.0), jnp.where(first, 0.0, weights)]
        return jnp.concatenate(wide, axis=1).astype(jnp.bfloat16), top, total

    def add_up(p, wide):
        outs = []
        for i in range(4):
            tile = jnp.dot(
                wide[16 * i : 16 * i + 16, :],
                values[2 * p : 2 * p + 2, :, 256 * i : 256 * i + 256].reshape(256, 256),
                preferred_element_type=jnp.float32,
            )
            outs.append(jnp.where(upper[0:16, :], tile[:, :128], tile[:, 128:]))
        return jnp.concatenate(outs, axis=0)

    def send(p, outs, top, total):
        outs = outs / total
        largest = jnp.max(jnp.abs(outs), axis=1, keepdims=True)
        power = jnp.ceil(jnp.log2(jnp.maximum(largest, 1e-30)))
        whole = jnp.round(outs * (jnp.exp2(-power) * TOP)).astype(jnp.int32).astype(jnp.int16)
        lse = top + jnp.log(total)
        coarse = jnp.round(lse * 16.0)
        fine = jnp.round((lse - coarse * 0.0625) * 524288.0)
        columns = []
        for kind in (coarse, fine, power):
            for i in range(0, 64, 16):
                pair = [jnp.broadcast_to(kind[i + n : i + n + 8, :], (8, 128)) for n in (0, 8)]
                columns.append(jnp.where(lanes[0:8] == 0, *pair))
        columns.append(jnp.zeros((32, 128), jnp.float32))
        lines = jnp.transpose(jnp.concatenate(columns, axis=0))[0:8, :]
        lines = lines.astype(jnp.int32).astype(jnp.int16)
        for n in range(2):
            target = targets[2 * p + n]
            block = jnp.concatenate([whole[i + 8 * n : i + 8 * n + 8] for i in range(0, 64, 16)], axis=0)
            for i in range(HQ // 2):
                out[target, i, :, :] = block[2 * i : 2 * i + 2, :]
            out[target, HQ // 2, :, :] = lines[n : n + 2, :]

    out[...] = jnp.zeros(out.shape, jnp.int16)
    scores = [score(0), score(1)]
    soft = [weigh(scores[0])]
    scores.append(score(2))
    sums = [add_up(0, soft[0][0])]
    soft.append(weigh(scores[1]))
    sums.append(add_up(1, soft[1][0]))
    soft.append(weigh(scores[2]))
    send(0, sums[0], *soft[0][1:])
    sums.append(add_up(2, soft[2][0]))
    send(1, sums[1], *soft[1][1:])
    send(2, sums[2], *soft[2][1:])


def statistics_tile(lse, power):
    row = iota((8, 128), 0)
    coarse = jnp.round(lse * 16.0)
    fine = jnp.round((lse - coarse * 0.0625) * 524288.0)
    tile = jnp.where(row == 0, coarse, jnp.where(row == 1, fine, jnp.where(row == 2, power, 0.0)))
    return tile.astype(jnp.int32).astype(jnp.int16)


def statistics(recv):
    tiles = recv[:, HQ:MESSAGE_ROWS, :].astype(jnp.int32).astype(jnp.float32)
    return tiles[:, 0, :] * 0.0625 + tiles[:, 1, :] * (1.0 / 524288.0), tiles[:, 2, :]


def merge_kernel(recv, member, out, sums_of):
    place = member[...]
    lines = [
        recv[SHORT_ROWS * g + HQ : SHORT_ROWS * (g + 1), :].astype(jnp.int32).astype(jnp.float32)[0:1]
        for g in range(32)
    ]
    tile = jnp.concatenate(lines, axis=0)
    lse = tile * 0.0625 + pltpu.roll(tile, 96, 1) * (1.0 / 524288.0)
    power = pltpu.roll(tile, 64, 1)
    peak, unit, total = (jnp.zeros((32, 128), jnp.float32) for _ in range(3))
    tops, units, sums = [], [], []
    for j in range(8):
        own = place == j
        tops.append(jnp.max(jnp.where(own, lse, ABSENT), axis=0, keepdims=True))
        units.append(jnp.max(jnp.where(own, power, -110.0), axis=0, keepdims=True))
        peak = jnp.where(own, tops[j], peak)
        unit = jnp.where(own, units[j], unit)
    weight = jnp.where(place >= 0.0, jnp.exp(lse - peak), 0.0)
    for j in range(8):
        own = place == j
        sums.append(jnp.sum(jnp.where(own, weight, 0.0), axis=0, keepdims=True))
        total = jnp.where(own, sums[j], total)
    total = jnp.where(place >= 0.0, total, 1.0)
    factor = jnp.transpose(weight / total * jnp.exp2(power - unit))[0:HQ, :]
    sums_of[...] = jnp.zeros(sums_of.shape, jnp.float32)
    for g in range(32):
        row = recv[SHORT_ROWS * g : SHORT_ROWS * g + HQ, :].astype(jnp.int32).astype(jnp.float32)
        row = row * jnp.broadcast_to(factor[:, g : g + 1], (HQ, 128))
        j = jnp.max(place[g : g + 1, 0:1]).astype(jnp.int32)
        j = jnp.where(j < 0, 8, j)
        sums_of[j + 9 * (g % 2)] = sums_of[j + 9 * (g % 2)] + row
    for j in range(8):
        out[j, 0:HQ, :] = jnp.round(sums_of[j] + sums_of[j + 9]).astype(jnp.int32).astype(jnp.int16)
        lse = jnp.where(sums[j] > 0.0, tops[j] + jnp.log(jnp.maximum(sums[j], 1e-30)), ABSENT)
        out[j, HQ:MESSAGE_ROWS, :] = statistics_tile(lse, units[j])


def finish_kernel(recv, out):
    lse, power = statistics(recv)
    weight = jnp.exp(lse - jnp.max(lse, axis=0, keepdims=True))
    total = jnp.sum(weight, axis=0, keepdims=True)
    factor = jnp.transpose(weight / total * (jnp.exp2(power) * (1.0 / TOP)))[0:HQ, :]
    acc = jnp.zeros((HQ, 128), jnp.float32)
    for k in range(8):
        row = recv[k, 0:HQ, :].astype(jnp.int32).astype(jnp.float32)
        acc = acc + row * jnp.broadcast_to(factor[:, k : k + 1], (HQ, 128))
    for h in range(HQ):
        out[0:1, 128 * h : 128 * h + 128] = acc[h : h + 1, :].astype(jnp.bfloat16)


VMEM = pl.BlockSpec(memory_space=pltpu.VMEM)
HBM = pl.BlockSpec(memory_space=pltpu.MemorySpace.HBM)


def kernel_call(kernel, shapes, in_specs, name, scratch=(), flops=None):
    return pl.pallas_call(
        kernel,
        out_shape=shapes,
        in_specs=in_specs,
        out_specs=jax.tree.map(lambda _: VMEM, shapes),
        scratch_shapes=scratch,
        name=name,
        cost_estimate=flops and pl.CostEstimate(flops, 0, 0),
        compiler_params=pltpu.CompilerParams(vmem_limit_bytes=32 * 1024 * 1024),
    )


def on_device(queries, paged_key_cache, paged_value_cache, page_request, page_number, lengths):
    shape = jax.ShapeDtypeStruct
    sent = kernel_call(
        spread_kernel,
        shape((512, 128), jnp.bfloat16),
        [HBM, HBM],
        "spread",
        scratch=[
            pltpu.SMEM((SLOTS,), jnp.int32),
            pltpu.VMEM((1, HQ * HEAD_SIZE), jnp.bfloat16),
            pltpu.SemaphoreType.DMA((2,)),
        ],
    )(
        pltpu.with_memory_space_constraint(page_request, pltpu.MemorySpace.HBM),
        pltpu.with_memory_space_constraint(queries, pltpu.MemorySpace.HBM),
    )
    heads = lax.all_to_all(sent, ("req", "kv"), 0, 0, tiled=True)
    picked, member = kernel_call(
        select_kernel,
        (shape((256, 128), jnp.bfloat16), shape((32, 128), jnp.float32)),
        [VMEM],
        "select",
        flops=10**10,
    )(heads)
    wanted = lax.all_to_all(picked, "req", 0, 0, tiled=True)
    partial = kernel_call(
        attend_kernel,
        shape((32, SHORT_ROWS // 2, 2, 128), jnp.int16),
        [VMEM] * 6,
        "attend",
    )(
        page_request.reshape(1, -1),
        page_number.reshape(1, -1),
        lengths.reshape(1, -1),
        wanted,
        paged_key_cache,
        paged_value_cache,
    )
    partial = lax.all_to_all(partial, "req", 0, 0, tiled=True).reshape(32 * SHORT_ROWS, 128)
    merged = kernel_call(
        merge_kernel,
        shape((8, MESSAGE_ROWS, 128), jnp.int16),
        [VMEM, VMEM],
        "merge",
        [pltpu.VMEM((18, HQ, 128), jnp.float32)],
    )(partial, member)
    merged = lax.all_to_all(merged, "kv", 0, 0, tiled=True)
    return kernel_call(finish_kernel, shape((1, 4096), jnp.bfloat16), [VMEM], "finish")(merged)


def solution(mesh):
    placed = (
        P(("req", "kv"), None),
        P(("req", "kv"), None, None),
        P(("req", "kv"), None, None),
        P(("req", "kv")),
        P(("req", "kv")),
        P(),
    )
    return jax.shard_map(
        on_device, mesh=mesh, in_specs=placed, out_specs=P(("req", "kv"), None), check_vma=False
    )
```

```python
import jax
import jax.numpy as jnp
from jax import lax
from jax.experimental import pallas as pl
from jax.experimental.pallas import tpu as pltpu
from jax.sharding import PartitionSpec as P

HQ = 32
HEAD_SIZE = 128
PAGE = 128
SLOTS = 6
MESSAGE_ROWS = 40
SHORT_ROWS = 34
ABSENT = -2048.0
TOP = 32767.0


def iota(shape, dim):
    return lax.broadcasted_iota(jnp.int32, shape, dim)


def spread_kernel(pages_in, query_in, out, pages, query, sems):
    first_copy = pltpu.make_async_copy(pages_in, pages, sems.at[0])
    second_copy = pltpu.make_async_copy(query_in, query, sems.at[1])
    first_copy.start()
    second_copy.start()
    first_copy.wait()
    lane = iota((16, 128), 1)
    even = iota((16, 128), 0) % 2 == 0
    first = (lax.axis_index("req") % 16) * SLOTS
    ids = jnp.zeros((16, 128), jnp.float32)
    for s in range(SLOTS):
        ids = jnp.where(lane == first + s, pages[s].astype(jnp.float32), ids)
    second_copy.wait()
    for h in range(HQ):
        head = query[0:1, h * 128 : (h + 1) * 128].astype(jnp.float32)
        block = jnp.where(even, jnp.broadcast_to(head, (16, 128)), ids)
        out[16 * h : 16 * h + 16, :] = block.astype(jnp.bfloat16)


def select_kernel(recv, out, member):
    rows = recv[...]
    group, plane = lax.axis_index("req"), lax.axis_index("kv")
    at, half = iota((8, 512), 1), iota((8, 512), 0)
    source = at // 2
    pick = (at % 2 == 1) & (source % 8 == plane) & (source // 128 == half)
    ids = jnp.dot(pick.astype(jnp.bfloat16), rows, preferred_element_type=jnp.float32)
    ids = ids.astype(jnp.int32)
    lane = iota((1, 128), 1)
    spots = []
    for n in range(2):
        wanted = ids[n : n + 1, :]
        hot = iota((512, 128), 0) == jnp.broadcast_to(2 * wanted, (512, 128))
        hot = hot.astype(jnp.float32).astype(jnp.bfloat16)
        got = lax.dot_general(
            hot, rows, (((0,), (0,)), ((), ())), preferred_element_type=jnp.float32
        )
        out[16 * SLOTS * n : 16 * SLOTS * (n + 1), :] = got[0 : 16 * SLOTS].astype(jnp.bfloat16)
        mine = (wanted // 8 == group) & (lane < 16 * SLOTS)
        spots.append(jnp.where(mine, wanted % 8 + 1, 0).astype(jnp.float32))
    dev, lanes = iota((32, 128), 0), iota((32, 128), 1)
    both = jnp.where(dev < 16, spots[0], spots[1])
    own = jnp.where(lanes // SLOTS == dev % 16, both, 0.0)
    place = jnp.sum(own, axis=1, keepdims=True) - 1.0
    member[...] = jnp.broadcast_to(place, (32, 128))


def attend_kernel(pages, numbers, lengths, recv, keys, values, out):
    whose, counts = pages[...], lengths[...].astype(jnp.float32)
    before = numbers[...].astype(jnp.float32) * PAGE
    request = iota(counts.shape, 1)
    limits, targets = [], []
    for s in range(SLOTS):
        own = request == whose[:, s : s + 1]
        count = jnp.sum(jnp.where(own, counts, 0.0), axis=1, keepdims=True)
        limits.append(jnp.broadcast_to(count - before[:, s : s + 1], (8, 128)))
        group = jnp.max(whose[:, s : s + 1].astype(jnp.float32)).astype(jnp.int32)
        targets.append(lax.shift_right_logical(group, 3))
    rows = SLOTS * HQ
    r, c = iota((rows, rows), 0), iota((rows, rows), 1)
    slot, head = r // 64 * 2 + r // 8 % 2, r // 16 % 4 * 8 + r % 8
    order = (c == head * SLOTS + slot).astype(jnp.float32).astype(jnp.bfloat16)
    query = jnp.dot(order, recv[...], preferred_element_type=jnp.float32)
    upper = iota((64, 128), 0) % 8 < 4
    first = iota((64, 128), 0) % 16 < 8
    lane = iota((8, 128), 1).astype(jnp.float32)
    lanes = iota((64, 128), 1)

    def score(p):
        rows = query[64 * p : 64 * p + 64, :]
        both = jnp.concatenate([jnp.where(upper, rows, 0.0), jnp.where(upper, 0.0, rows)], axis=1)
        both = both.astype(jnp.bfloat16)
        scores = []
        for i in range(4):
            tile = lax.dot_general(
                both[16 * i : 16 * i + 16, :],
                keys[2 * p : 2 * p + 2, :, 256 * i : 256 * i + 256].reshape(256, 256),
                (((1,), (1,)), ((), ())),
                preferred_element_type=jnp.float32,
            )
            for n in range(2):
                part = tile[8 * n : 8 * n + 8, 128 * n : 128 * n + 128] * HEAD_SIZE**-0.5
                scores.append(jnp.where(lane < limits[2 * p + n], part, -1e30))
        return jnp.concatenate(scores, axis=0)

    def weigh(scores):
        top = jnp.max(scores, axis=1, keepdims=True)
        weights = jnp.exp(scores - top)
        total = jnp.sum(weights, axis=1, keepdims=True)
        wide = [jnp.where(first, weights, 0.0), jnp.where(first, 0.0, weights)]
        return jnp.concatenate(wide, axis=1).astype(jnp.bfloat16), top, total

    def add_up(p, wide):
        outs = []
        for i in range(4):
            tile = jnp.dot(
                wide[16 * i : 16 * i + 16, :],
                values[2 * p : 2 * p + 2, :, 256 * i : 256 * i + 256].reshape(256, 256),
                preferred_element_type=jnp.float32,
            )
            outs.append(jnp.where(upper[0:16, :], tile[:, :128], tile[:, 128:]))
        return jnp.concatenate(outs, axis=0)

    def send(p, outs, top, total):
        outs = outs / total
        largest = jnp.max(jnp.abs(outs), axis=1, keepdims=True)
        power = jnp.ceil(jnp.log2(jnp.maximum(largest, 1e-30)))
        whole = jnp.round(outs * (jnp.exp2(-power) * TOP)).astype(jnp.int32).astype(jnp.int16)
        lse = top + jnp.log(total)
        coarse = jnp.round(lse * 16.0)
        fine = jnp.round((lse - coarse * 0.0625) * 524288.0)
        columns = []
        for kind in (coarse, fine, power):
            for i in range(0, 64, 16):
                pair = [jnp.broadcast_to(kind[i + n : i + n + 8, :], (8, 128)) for n in (0, 8)]
                columns.append(jnp.where(lanes[0:8] == 0, *pair))
        columns.append(jnp.zeros((32, 128), jnp.float32))
        lines = jnp.transpose(jnp.concatenate(columns, axis=0))[0:8, :]
        lines = lines.astype(jnp.int32).astype(jnp.int16)
        for n in range(2):
            target = targets[2 * p + n]
            block = jnp.concatenate([whole[i + 8 * n : i + 8 * n + 8] for i in range(0, 64, 16)], axis=0)
            for i in range(HQ // 2):
                out[target, i, :, :] = block[2 * i : 2 * i + 2, :]
            out[target, HQ // 2, :, :] = lines[n : n + 2, :]

    out[...] = jnp.zeros(out.shape, jnp.int16)
    scores = [score(0), score(1)]
    soft = [weigh(scores[0])]
    scores.append(score(2))
    sums = [add_up(0, soft[0][0])]
    soft.append(weigh(scores[1]))
    sums.append(add_up(1, soft[1][0]))
    soft.append(weigh(scores[2]))
    send(0, sums[0], *soft[0][1:])
    sums.append(add_up(2, soft[2][0]))
    send(1, sums[1], *soft[1][1:])
    send(2, sums[2], *soft[2][1:])


def statistics_tile(lse, power):
    row = iota((8, 128), 0)
    coarse = jnp.round(lse * 16.0)
    fine = jnp.round((lse - coarse * 0.0625) * 524288.0)
    tile = jnp.where(row == 0, coarse, jnp.where(row == 1, fine, jnp.where(row == 2, power, 0.0)))
    return tile.astype(jnp.int32).astype(jnp.int16)


def statistics(recv):
    tiles = recv[:, HQ:MESSAGE_ROWS, :].astype(jnp.int32).astype(jnp.float32)
    return tiles[:, 0, :] * 0.0625 + tiles[:, 1, :] * (1.0 / 524288.0), tiles[:, 2, :]


def merge_kernel(recv, member, out, sums_of):
    place = member[...]
    lines = [
        recv[SHORT_ROWS * g + HQ : SHORT_ROWS * (g + 1), :].astype(jnp.int32).astype(jnp.float32)[0:1]
        for g in range(32)
    ]
    tile = jnp.concatenate(lines, axis=0)
    lse = tile * 0.0625 + pltpu.roll(tile, 96, 1) * (1.0 / 524288.0)
    power = pltpu.roll(tile, 64, 1)
    peak, unit, total = (jnp.zeros((32, 128), jnp.float32) for _ in range(3))
    tops, units, sums = [], [], []
    for j in range(8):
        own = place == j
        tops.append(jnp.max(jnp.where(own, lse, ABSENT), axis=0, keepdims=True))
        units.append(jnp.max(jnp.where(own, power, -110.0), axis=0, keepdims=True))
        peak = jnp.where(own, tops[j], peak)
        unit = jnp.where(own, units[j], unit)
    weight = jnp.where(place >= 0.0, jnp.exp(lse - peak), 0.0)
    for j in range(8):
        own = place == j
        sums.append(jnp.sum(jnp.where(own, weight, 0.0), axis=0, keepdims=True))
        total = jnp.where(own, sums[j], total)
    total = jnp.where(place >= 0.0, total, 1.0)
    factor = jnp.transpose(weight / total * jnp.exp2(power - unit))[0:HQ, :]
    sums_of[...] = jnp.zeros(sums_of.shape, jnp.float32)
    for g in range(32):
        row = recv[SHORT_ROWS * g : SHORT_ROWS * g + HQ, :].astype(jnp.int32).astype(jnp.float32)
        row = row * jnp.broadcast_to(factor[:, g : g + 1], (HQ, 128))
        j = jnp.max(place[g : g + 1, 0:1]).astype(jnp.int32)
        j = jnp.where(j < 0, 8, j)
        sums_of[j + 9 * (g % 2)] = sums_of[j + 9 * (g % 2)] + row
    for j in range(8):
        out[j, 0:HQ, :] = jnp.round(sums_of[j] + sums_of[j + 9]).astype(jnp.int32).astype(jnp.int16)
        lse = jnp.where(sums[j] > 0.0, tops[j] + jnp.log(jnp.maximum(sums[j], 1e-30)), ABSENT)
        out[j, HQ:MESSAGE_ROWS, :] = statistics_tile(lse, units[j])


def finish_kernel(recv, out):
    lse, power = statistics(recv)
    weight = jnp.exp(lse - jnp.max(lse, axis=0, keepdims=True))
    total = jnp.sum(weight, axis=0, keepdims=True)
    factor = jnp.transpose(weight / total * (jnp.exp2(power) * (1.0 / TOP)))[0:HQ, :]
    acc = jnp.zeros((HQ, 128), jnp.float32)
    for k in range(8):
        row = recv[k, 0:HQ, :].astype(jnp.int32).astype(jnp.float32)
        acc = acc + row * jnp.broadcast_to(factor[:, k : k + 1], (HQ, 128))
    for h in range(HQ):
        out[0:1, 128 * h : 128 * h + 128] = acc[h : h + 1, :].astype(jnp.bfloat16)


VMEM = pl.BlockSpec(memory_space=pltpu.VMEM)
HBM = pl.BlockSpec(memory_space=pltpu.MemorySpace.HBM)


def kernel_call(kernel, shapes, in_specs, name, scratch=(), flops=None):
    return pl.pallas_call(
        kernel,
        out_shape=shapes,
        in_specs=in_specs,
        out_specs=jax.tree.map(lambda _: VMEM, shapes),
        scratch_shapes=scratch,
        name=name,
        cost_estimate=flops and pl.CostEstimate(flops, 0, 0),
        compiler_params=pltpu.CompilerParams(vmem_limit_bytes=32 * 1024 * 1024),
    )


def on_device(queries, paged_key_cache, paged_value_cache, page_request, page_number, lengths):
    shape = jax.ShapeDtypeStruct
    sent = kernel_call(
        spread_kernel,
        shape((512, 128), jnp.bfloat16),
        [HBM, HBM],
        "spread",
        scratch=[
            pltpu.SMEM((SLOTS,), jnp.int32),
            pltpu.VMEM((1, HQ * HEAD_SIZE), jnp.bfloat16),
            pltpu.SemaphoreType.DMA((2,)),
        ],
    )(
        pltpu.with_memory_space_constraint(page_request, pltpu.MemorySpace.HBM),
        pltpu.with_memory_space_constraint(queries, pltpu.MemorySpace.HBM),
    )
    heads = lax.all_to_all(sent, ("req", "kv"), 0, 0, tiled=True)
    picked, member = kernel_call(
        select_kernel,
        (shape((HQ * SLOTS, 128), jnp.bfloat16), shape((32, 128), jnp.float32)),
        [VMEM],
        "select",
        flops=10**10,
    )(heads)
    picked = picked.reshape(HQ, SLOTS // 2, 2, 128)
    wanted = lax.all_to_all(picked, "req", 0, 0, tiled=True).reshape(HQ * SLOTS, 128)
    partial = kernel_call(
        attend_kernel,
        shape((32, SHORT_ROWS // 2, 2, 128), jnp.int16),
        [VMEM] * 6,
        "attend",
    )(
        page_request.reshape(1, -1),
        page_number.reshape(1, -1),
        lengths.reshape(1, -1),
        wanted,
        paged_key_cache,
        paged_value_cache,
    )
    partial = lax.all_to_all(partial, "req", 0, 0, tiled=True).reshape(32 * SHORT_ROWS, 128)
    merged = kernel_call(
        merge_kernel,
        shape((8, MESSAGE_ROWS, 128), jnp.int16),
        [VMEM, VMEM],
        "merge",
        [pltpu.VMEM((18, HQ, 128), jnp.float32)],
    )(partial, member)
    merged = lax.all_to_all(merged, "kv", 0, 0, tiled=True)
    return kernel_call(finish_kernel, shape((1, 4096), jnp.bfloat16), [VMEM], "finish")(merged)


def solution(mesh):
    placed = (
        P(("req", "kv"), None),
        P(("req", "kv"), None, None),
        P(("req", "kv"), None, None),
        P(("req", "kv")),
        P(("req", "kv")),
        P(),
    )
    return jax.shard_map(
        on_device, mesh=mesh, in_specs=placed, out_specs=P(("req", "kv"), None), check_vma=False
    )
```
